32 devices in a mesh: fsdp: 8 (over z, y), seq: 4 (over x, core).
Axes of the slice: x: 2, y: 2, z: 4, core: 2. Of those that a mesh axis runs over, the one named last changes fastest.
Arguments:
- activations: bfloat16 [8, 2560, 1024], P('fsdp', 'seq'), may hold values from -6 to 6
- cotangent: bfloat16 [8, 2560, 1024], P('fsdp', 'seq'), may hold values from -6 to 6
- gain_attn: bfloat16 [1024], P('fsdp'), may hold values from 0.25 to 1.75
- w_qkv: bfloat16 [1024, 3072], P('fsdp'), may hold values from -0.25 to 0.25
- w_attn_out: bfloat16 [1024, 1024], P('fsdp'), may hold values from -0.75 to 0.75
- gain_mlp: bfloat16 [1024], P('fsdp'), may hold values from 0.25 to 1.75
- w_in: bfloat16 [1024, 5248], P('fsdp'), may hold values from -0.1875 to 0.1875
- w_mlp_out: bfloat16 [2624, 1024], P('fsdp'), may hold values from -0.125 to 0.125
Outputs:
- output: bfloat16 [8, 2560, 1024], P('fsdp', 'seq')
- d_input: bfloat16 [8, 2560, 1024], P('fsdp', 'seq')
- grad_gain_attn: float32 [1024], P('fsdp')
- grad_gain_mlp: float32 [1024], P('fsdp')
- grad_w_qkv: float32 [1024, 3072], P('fsdp')
- grad_w_attn_out: float32 [1024, 1024], P('fsdp')
- grad_w_in: float32 [1024, 5248], P('fsdp')
- grad_w_mlp_out: float32 [2624, 1024], P('fsdp')
The draws below stay inside these ranges and needn't reach their ends.
All inputs are finite; a program needn't handle non-finite values.
Results may differ from the reference program's by a relative error of at most 0.023.
Values may be sent and summed in bfloat16 or wider, within the bound.
No kernel may reach another device: no remote copies, remote signals or barrier semaphores. Data moves between devices by JAX's collectives and lax.ppermute only.
A program may use at most 192 MiB of HBM per device.

```python
import math
import jax
import jax.numpy as jnp
from jax import lax

D = 1024
HEADS = 16
HEAD = 64
FF = 2624
LENGTH = 2560
QB = 512
SEQS = 8


def shard_levels(rng, dims, split, least, largest):
    gain = 1.0
    for axis_at, blocks in split:
        draws = jax.random.uniform(jax.random.fold_in(jax.random.fold_in(rng, 6), axis_at), (blocks,), jnp.float32, least / len(split), largest / len(split))
        gain = gain * jnp.repeat(jnp.exp(draws), dims[axis_at] // blocks).reshape((-1,) + (1,) * (len(dims) - 1 - axis_at))
    return gain


def normal_values(stream_key, extent, scale, bound, cuts=(), kind=jnp.bfloat16):
    loudness = shard_levels(stream_key, extent, cuts, -0.22, 0.18) if cuts else 1.0
    drawn = jax.random.normal(stream_key, extent, jnp.float32) * scale * loudness
    return jnp.minimum(jnp.maximum(drawn, -bound), bound).astype(kind)


def setup_inputs(seed: int = 0) -> dict:
    splits = jax.random.split(jax.random.key(seed), 9)
    activations = normal_values(splits[0], (SEQS, LENGTH, D), 1.0, 6.0, ((0, 8), (1, 4)))
    cotangent = normal_values(splits[1], (SEQS, LENGTH, D), 1.0, 6.0, ((0, 8), (1, 4)))
    gain_attn = jnp.clip(1.0 + 0.15 * jax.random.normal(splits[2], (D,), jnp.float32), 0.25, 1.75).astype(jnp.bfloat16)
    w_qkv = normal_values(splits[3], (D, 3 * D), (D // 2) ** -0.5, 0.25, ((0, 8),))
    w_attn_out = normal_values(splits[4], (D, D), (D // 16) ** -0.5, 0.75, ((0, 8),))
    gain_mlp = jnp.clip(1.0 + 0.15 * jax.random.normal(splits[5], (D,), jnp.float32), 0.25, 1.75).astype(jnp.bfloat16)
    w_in = normal_values(splits[6], (D, 2 * FF), D ** -0.5, 0.1875, ((0, 8),))
    w_mlp_out = normal_values(splits[7], (FF, D), FF ** -0.5, 0.125, ((0, 8),))
    return {"activations": activations, "cotangent": cotangent, "gain_attn": gain_attn, "w_qkv": w_qkv, "w_attn_out": w_attn_out, "gain_mlp": gain_mlp, "w_in": w_in, "w_mlp_out": w_mlp_out}


eps = 1e-05
rope_base = 160000.0
highest = lax.Precision.HIGHEST

@jax.custom_vjp
def low(v):
    return lax.optimization_barrier(v.astype(jnp.bfloat16)).astype(jnp.float32)

@jax.custom_vjp
def low_back(v):
    return v

def low_keep(v):
    return (low(v), None)

def low_pass(kept, grad):
    return (grad,)

def back_keep(v):
    return (v, None)

def back_low(kept, grad):
    return (low(grad),)
low.defvjp(low_keep, low_pass)
low_back.defvjp(back_keep, back_low)

def layer_norm(values, gain_vec):
    average = lax.optimization_barrier(jnp.mean(values, -1, keepdims=True))
    centred = values - average
    variance = lax.optimization_barrier(jnp.mean(centred * centred, -1, keepdims=True))
    return centred * lax.rsqrt(variance + eps) * gain_vec

def gelu_exact(values):
    return 0.5 * values * (1.0 + lax.erf(values * 2.0 ** (-0.5)))

def rope_tables(positions):
    half_size = HEAD // 2
    freq_index = jnp.arange(half_size).astype(positions.dtype)
    inverse = jnp.exp(freq_index * (-2.0 * math.log(rope_base) / HEAD))
    angles = positions[:, None] * inverse[None, :]
    angles = jnp.concatenate([angles, angles], 1)
    return (jnp.cos(angles), jnp.sin(angles))

def rotate(tensor, cosine, sine_table):
    half_size = HEAD // 2
    first = tensor[..., :half_size]
    second = tensor[..., half_size:]
    turned = jnp.concatenate([-second, first], -1)
    return tensor * cosine + turned * sine_table

def attend_block(q_block, key_rows, value_rows):
    scores = low_back(jnp.einsum('qhd,khd->hqk', q_block, key_rows, precision=highest) * float(HEAD) ** (-0.5))
    row_peak = lax.optimization_barrier(jnp.max(scores, -1, keepdims=True))
    exponent = jnp.exp(scores - row_peak)
    probs = low(exponent / lax.optimization_barrier(jnp.sum(exponent, -1, keepdims=True)))
    return low_back(low(jnp.einsum('hqk,khd->qhd', probs, value_rows, precision=highest)))

def layer_forward(tokens, gain_attn, w_qkv, w_attn_out, gain_mlp, w_in, w_mlp_out):
    normed = low(layer_norm(tokens, gain_attn))
    packed = low_back(jnp.dot(normed, w_qkv, precision=highest)).reshape(LENGTH, 3, HEADS, HEAD)
    cosine, sine_table = rope_tables(jnp.arange(LENGTH).astype(tokens.dtype))
    turned = rotate(packed[:, :2], cosine[:, None, None, :], sine_table[:, None, None, :])
    rotated = low_back(low(jnp.concatenate([turned, packed[:, 2:]], 1)))
    queries = rotated[:, 0].reshape(LENGTH // QB, QB, HEADS, HEAD)
    key_rows = rotated[:, 1]
    value_rows = rotated[:, 2]
    attended = lax.map(lambda q_block: jax.checkpoint(attend_block)(q_block, key_rows, value_rows), queries)
    attended = attended.reshape(LENGTH, D)
    mixed = tokens + low_back(jnp.dot(attended, w_attn_out, precision=highest))
    normed_mlp = low(layer_norm(mixed, gain_mlp))
    gate_up = low_back(jnp.dot(normed_mlp, w_in, precision=highest))
    hidden = low(gelu_exact(gate_up[:, :FF]) * gate_up[:, FF:])
    return mixed + low_back(jnp.dot(hidden, w_mlp_out, precision=highest))

def reference(activations, cotangent, gain_attn, w_qkv, w_attn_out, gain_mlp, w_in, w_mlp_out):
    weights = (gain_attn.astype(jnp.float32), w_qkv.astype(jnp.float32), w_attn_out.astype(jnp.float32), gain_mlp.astype(jnp.float32), w_in.astype(jnp.float32), w_mlp_out.astype(jnp.float32))
    starting = tuple((jnp.zeros(member.shape, jnp.float32) for member in weights))

    def advance(running, pieces):
        sequence, incoming = pieces
        result, pullback = jax.vjp(layer_forward, sequence.astype(jnp.float32), *weights)
        gradients = pullback(incoming.astype(jnp.float32))
        running = tuple((summed + grad_part for summed, grad_part in zip(running, gradients[1:])))
        return (running, (result.astype(jnp.bfloat16), gradients[0].astype(jnp.bfloat16)))
    running, (outputs, input_grads) = lax.scan(advance, starting, (activations, cotangent))
    return (outputs, input_grads, running[0], running[3], running[1], running[2], running[4], running[5])
```

```python
import functools
import math

import jax
import jax.numpy as jnp
from jax import lax
from jax.experimental import pallas as pl
from jax.experimental.pallas import tpu as pltpu
from jax.sharding import PartitionSpec as P

HEADS = 16
HEAD = 64
HALF = HEAD // 2
ROW_TILE = 16
BF16 = jnp.bfloat16
F32 = jnp.float32

eps = 1e-05
rope_base = 160000.0
VMEM_BYTES = 60 << 20


def dot_nn(a, b):
    return lax.dot_general(a, b, (((1,), (0,)), ((), ())), preferred_element_type=F32)


def dot_nt(a, b):
    return lax.dot_general(a, b, (((1,), (1,)), ((), ())), preferred_element_type=F32)


def dot_tn(a, b):
    return lax.dot_general(a, b, (((0,), (0,)), ((), ())), preferred_element_type=F32)


def block_rows(rows, wanted):
    best = rows
    for size in range(ROW_TILE, min(rows, wanted) + 1, ROW_TILE):
        if rows % size == 0:
            best = size
    return best


def centred_stats(values):
    average = jnp.mean(values, -1, keepdims=True)
    centred = values - average
    inverse = lax.rsqrt(jnp.mean(centred * centred, -1, keepdims=True) + eps)
    return centred * inverse, inverse


def norm_backward(grad, xhat, inverse):
    return inverse * (
        grad
        - jnp.mean(grad, -1, keepdims=True)
        - xhat * jnp.mean(grad * xhat, -1, keepdims=True)
    )


def partner(values):
    width = values.shape[-1]
    if width % 128:
        return jnp.concatenate([values[:, HALF:], values[:, :HALF]], 1)
    lane = lax.broadcasted_iota(jnp.int32, values.shape, 1)
    return jnp.where(
        lane % HEAD < HALF,
        pltpu.roll(values, width - HALF, 1),
        pltpu.roll(values, HALF, 1),
    )


def widen(table, width):
    return jnp.concatenate([table] * (width // table.shape[1]), 1)


def head_of_lane(shape):
    return lax.broadcasted_iota(jnp.int32, shape, 1) // HEAD


def only_head(values, head):
    return jnp.where(head_of_lane(values.shape) == head, values, jnp.zeros_like(values))


def qkv_body(x_ref, w_ref, cos_ref, sin_ref, q_ref, k_ref, v_ref):
    width = q_ref.shape[1]
    packed = dot_nn(x_ref[...], w_ref[...])
    cosine = widen(cos_ref[...], width)
    sine = widen(sin_ref[...], width)
    for at, ref in enumerate((q_ref, k_ref)):
        part = packed[:, at * width : (at + 1) * width]
        ref[...] = (part * cosine + partner(part) * sine).astype(BF16)
    v_ref[...] = packed[:, 2 * width :].astype(BF16)


def qkv_heads(x, weights, cosine, sine):
    rows, depth = x.shape
    width = weights.shape[1] // 3
    step = block_rows(rows, 512)
    table = cosine.shape[1]
    by_row = lambda columns: pl.BlockSpec((step, columns), lambda i: (i, 0))
    return pl.pallas_call(
        qkv_body,
        grid=(rows // step,),
        in_specs=[
            by_row(depth),
            pl.BlockSpec((depth, 3 * width), lambda i: (0, 0)),
            by_row(table),
            by_row(table),
        ],
        out_specs=[by_row(width)] * 3,
        out_shape=[jax.ShapeDtypeStruct((rows, width), BF16)] * 3,
        compiler_params=pltpu.CompilerParams(vmem_limit_bytes=VMEM_BYTES),
        cost_estimate=pl.CostEstimate(
            flops=6 * rows * depth * width,
            bytes_accessed=2 * (rows * depth + 3 * depth * width + 3 * rows * width),
            transcendentals=0,
        ),
        name="qkv_rope",
    )(x, weights, cosine, sine)


def attend_body(q_ref, k_ref, v_ref, out_ref, lse_ref):
    width = q_ref.shape[1]
    queries = q_ref[...] * jnp.asarray(HEAD**-0.5, BF16)
    keys = k_ref[...]
    values = v_ref[...]
    for head in range(width // HEAD):
        scores = dot_nt(only_head(queries, head), keys)
        peak = jnp.max(scores, -1, keepdims=True)
        exponent = jnp.exp(scores - peak)
        total = jnp.sum(exponent, -1, keepdims=True)
        out = dot_nn(exponent.astype(BF16), values) / total
        lse = jnp.broadcast_to(peak + jnp.log(total), out.shape)
        if head:
            here = head_of_lane(out.shape) == head
            out = jnp.where(here, out, previous_out)
            lse = jnp.where(here, lse, previous_lse)
        previous_out, previous_lse = out, lse
    out_ref[...] = out.astype(BF16)
    lse_ref[...] = lse.T


def attend(queries, keys, values):
    rows, local_width = queries.shape
    width = min(128, local_width)
    step = block_rows(rows, 256)
    q_spec = pl.BlockSpec((step, width), lambda g, i: (i, g))
    k_spec = pl.BlockSpec((rows, width), lambda g, i: (0, g))
    return pl.pallas_call(
        attend_body,
        grid=(local_width // width, rows // step),
        in_specs=[q_spec, k_spec, k_spec],
        out_specs=[q_spec, pl.BlockSpec((width, step), lambda g, i: (g, i))],
        out_shape=[
            jax.ShapeDtypeStruct((rows, local_width), BF16),
            jax.ShapeDtypeStruct((local_width, rows), F32),
        ],
        compiler_params=pltpu.CompilerParams(vmem_limit_bytes=VMEM_BYTES),
        cost_estimate=pl.CostEstimate(
            flops=16 * rows * rows * local_width,
            bytes_accessed=8 * rows * local_width,
            transcendentals=rows * rows * local_width // HEAD,
        ),
        name="attend",
    )(queries, keys, values)


def attend_back_body(
    q_ref, k_ref, v_ref, g_ref, out_ref, lse_ref, cos_ref, sin_ref, cos_all_ref, sin_all_ref,
    dq_ref, dk_ref, dv_ref, dk_sum, dv_sum,
):
    width = q_ref.shape[1]
    step = pl.program_id(1)

    @pl.when(step == 0)
    def _():
        dk_sum[...] = jnp.zeros_like(dk_sum)
        dv_sum[...] = jnp.zeros_like(dv_sum)

    factor = HEAD**-0.5
    queries = q_ref[...] * jnp.asarray(factor, BF16)
    keys = k_ref[...]
    values = v_ref[...]
    grads = g_ref[...]
    product = (grads.astype(F32) * out_ref[...].astype(F32)).T
    dq = jnp.zeros(product.shape, F32)
    for head in range(width // HEAD):
        own_queries = only_head(queries, head)
        own_grads = only_head(grads, head)
        lse = lse_ref[head * HEAD : head * HEAD + 1, :]
        inner = jnp.sum(product[head * HEAD : (head + 1) * HEAD], 0, keepdims=True)
        probs = jnp.exp(dot_nt(keys, own_queries) - lse)
        prob_grad = dot_nt(values, own_grads)
        score_grad = (probs * (prob_grad - inner)).astype(BF16)
        dv_sum[...] += dot_nn(probs.astype(BF16), own_grads)
        dk_sum[...] += dot_nn(score_grad, own_queries)
        dq = dq + dot_tn(only_head(keys, head), score_grad)
    dq = (dq.T * factor).astype(BF16).astype(F32)
    dq_ref[...] = (dq * cos_ref[...] - partner(dq) * sin_ref[...]).astype(BF16)

    @pl.when(step == pl.num_programs(1) - 1)
    def _():
        dk = dk_sum[...].astype(BF16).astype(F32)
        dk_ref[...] = (dk * cos_all_ref[...] - partner(dk) * sin_all_ref[...]).astype(BF16)
        dv_ref[...] = dv_sum[...].astype(BF16)


def attend_back(queries, keys, values, grads, out, lse, cosine, sine):
    rows, local_width = queries.shape
    width = min(128, local_width)
    step = block_rows(rows, 512)
    q_spec = pl.BlockSpec((step, width), lambda g, i: (i, g))
    k_spec = pl.BlockSpec((rows, width), lambda g, i: (0, g))
    t_spec = pl.BlockSpec((step, width), lambda g, i: (i, 0))
    all_spec = pl.BlockSpec((rows, width), lambda g, i: (0, 0))
    return pl.pallas_call(
        attend_back_body,
        grid=(local_width // width, rows // step),
        in_specs=[
            q_spec, k_spec, k_spec, q_spec, q_spec,
            pl.BlockSpec((width, step), lambda g, i: (g, i)),
            t_spec, t_spec, all_spec, all_spec,
        ],
        out_specs=[q_spec, k_spec, k_spec],
        out_shape=[jax.ShapeDtypeStruct((rows, local_width), BF16)] * 3,
        scratch_shapes=[pltpu.VMEM((rows, width), F32)] * 2,
        compiler_params=pltpu.CompilerParams(vmem_limit_bytes=VMEM_BYTES),
        cost_estimate=pl.CostEstimate(
            flops=40 * rows * rows * local_width,
            bytes_accessed=20 * rows * local_width,
            transcendentals=rows * rows * local_width // HEAD,
        ),
        name="attend_back",
    )(queries, keys, values, grads, out, lse, cosine, sine, cosine, sine)


def mlp_body(x_ref, c_ref, wi_ref, wo_ref, hidden_ref, gate_up_ref, back_ref, out_ref):
    units = wo_ref.shape[0]
    gate_up = dot_nn(x_ref[...], wi_ref[...])
    hidden_grad = dot_nt(c_ref[...], wo_ref[...])
    gate = gate_up[:, :units]
    up = gate_up[:, units:]
    share = 0.5 * (1.0 + lax.erf(gate * 2.0**-0.5))
    activated = gate * share
    slope = share + gate * jnp.exp(-0.5 * gate * gate) * (2.0 * math.pi) ** -0.5
    hidden = (activated * up).astype(BF16)
    hidden_ref[...] = hidden
    gate_grad = (hidden_grad * up * slope).astype(BF16)
    up_grad = (hidden_grad * activated).astype(BF16)
    both = jnp.concatenate([gate_grad, up_grad], 1)
    gate_up_ref[...] = both
    back_ref[...] = dot_nt(both, wi_ref[...]).astype(BF16)
    out_ref[...] = dot_nn(hidden, wo_ref[...]).astype(BF16)


def mlp(x, cotangent, w_in, w_out):
    rows, depth = x.shape
    units = w_out.shape[0]
    step = block_rows(rows, 320)
    by_row = lambda columns: pl.BlockSpec((step, columns), lambda i: (i, 0))
    whole = lambda shape: pl.BlockSpec(shape, lambda i: (0, 0))
    return pl.pallas_call(
        mlp_body,
        grid=(rows // step,),
        in_specs=[by_row(depth), by_row(depth), whole(w_in.shape), whole(w_out.shape)],
        out_specs=[by_row(units), by_row(2 * units), by_row(depth), by_row(depth)],
        out_shape=[
            jax.ShapeDtypeStruct((rows, columns), BF16)
            for columns in (units, 2 * units, depth, depth)
        ],
        compiler_params=pltpu.CompilerParams(vmem_limit_bytes=VMEM_BYTES),
        cost_estimate=pl.CostEstimate(
            flops=12 * rows * depth * units,
            bytes_accessed=2 * rows * (4 * depth + 3 * units) + 6 * depth * units,
            transcendentals=2 * rows * units,
        ),
        name="mlp",
    )(x, cotangent, w_in, w_out)


def local(seq_size, fsdp_size, activations, cotangent, gain_attn, w_qkv, w_attn_out, gain_mlp, w_in, w_mlp_out):
    _, positions, width = activations.shape
    shard = w_qkv.shape[0]
    ff_shard = w_mlp_out.shape[0]
    local_width = width // seq_size
    length = positions * seq_size
    me = lax.axis_index("seq")
    row = lax.axis_index("fsdp")

    bits = []
    bit = seq_size // 2
    while bit:
        bits.append(bit)
        bit //= 2
    order = [0]
    for bit in bits:
        order = order + [member ^ bit for member in order]

    def swap(values, axis, size, offset):
        return lax.ppermute(values, axis, [(i, i ^ offset) for i in range(size)])

    def gather_seq(values):
        pieces = [values]
        for bit in bits:
            pieces = pieces + [swap(piece, "seq", seq_size, bit) for piece in pieces]
        return pieces

    def scatter_seq(pieces):
        for bit in reversed(bits):
            half = len(pieces) // 2
            sent = [swap(piece, "seq", seq_size, bit) for piece in pieces[half:]]
            pieces = [
                (kept.astype(F32) + got.astype(F32)).astype(BF16)
                if half > 1
                else kept.astype(F32) + got.astype(F32)
                for kept, got in zip(pieces[:half], sent)
            ]
        return pieces[0]

    def exchange_seq(pieces):
        return [
            swap(piece, "seq", seq_size, offset) if offset else piece
            for piece, offset in zip(pieces, order)
        ]

    def by_member(pieces):
        stacked = jnp.stack(pieces)
        slots = jnp.asarray([order.index(member) for member in range(seq_size)])
        return [
            lax.dynamic_index_in_dim(stacked, slots[me ^ member], 0, keepdims=False)
            for member in range(seq_size)
        ]

    def gather_fsdp(values):
        rows = values.shape[0]
        gathered = values
        at = 0
        bit = fsdp_size // 2
        while bit:
            other = swap(gathered, "fsdp", fsdp_size, bit)
            high = (row & bit) != 0
            gathered = jnp.stack(
                [jnp.where(high, other, gathered), jnp.where(high, gathered, other)], at
            )
            at += 1
            bit //= 2
        return gathered.reshape(fsdp_size * rows, values.shape[1])

    def scatter_fsdp(values):
        rows = values.shape[0] // fsdp_size
        bit = 1
        left = values.reshape(fsdp_size // 2, 2, rows, values.shape[1])
        while True:
            mine = jnp.where((row & bit) != 0, 1, 0)
            kept = lax.dynamic_index_in_dim(left, mine, 1, keepdims=False)
            sent = lax.dynamic_index_in_dim(left, 1 - mine, 1, keepdims=False)
            total = kept.astype(F32) + swap(sent, "fsdp", fsdp_size, bit).astype(F32)
            bit *= 2
            if bit == fsdp_size:
                return total[0]
            left = total.astype(BF16).reshape(fsdp_size // (2 * bit), 2, rows, values.shape[1])

    own_gain_attn = gain_attn.astype(F32)[:, None]
    own_gain_mlp = gain_mlp.astype(F32)[:, None]

    qkv_slice = jnp.concatenate(
        [
            lax.dynamic_slice(w_qkv, (0, part * width + me * local_width), (shard, local_width))
            for part in range(3)
        ],
        1,
    )
    qkv_slice = (qkv_slice.astype(F32) * own_gain_attn).astype(BF16)
    qkv_full = gather_fsdp(qkv_slice)

    tokens = activations.reshape(positions, width).astype(F32)
    xhat, inverse = centred_stats(tokens)
    x_all = jnp.concatenate(gather_seq(xhat.astype(BF16)), 0)

    out_rows = shard // seq_size
    attn_out_slice = lax.dynamic_slice(w_attn_out, (me * out_rows, 0), (out_rows, width))
    attn_out_full = lax.all_gather(attn_out_slice, ("fsdp", "seq"), axis=0, tiled=True)

    unit_share = -(-ff_shard // seq_size)
    unit_share = -(-unit_share // ROW_TILE) * ROW_TILE
    padding = unit_share * seq_size - ff_shard
    units = fsdp_size * unit_share
    mlp_out_slice = lax.dynamic_slice(
        jnp.pad(w_mlp_out, ((0, padding), (0, 0))), (me * unit_share, 0), (unit_share, width)
    )
    in_slice = jnp.pad(
        w_in.reshape(shard, 2 * fsdp_size, ff_shard), ((0, 0), (0, 0), (0, padding))
    )
    in_slice = lax.dynamic_slice(
        in_slice, (0, 0, me * unit_share), (shard, 2 * fsdp_size, unit_share)
    ).reshape(shard, 2 * units)
    in_slice = (in_slice.astype(F32) * own_gain_mlp).astype(BF16)
    in_full = lax.all_gather(in_slice, "fsdp", axis=0, tiled=True)
    mlp_out_full = lax.all_gather(mlp_out_slice, "fsdp", axis=0, tiled=True)

    table = min(128, local_width)
    lane = lax.broadcasted_iota(jnp.int32, (length, table), 1)
    at = lax.broadcasted_iota(jnp.int32, (length, table), 0)
    members = jnp.asarray(order)[:, None, None] ^ me
    place = (members * positions + at.reshape(seq_size, positions, table) % positions).reshape(
        length, table
    )
    frequency = jnp.exp((lane % HALF).astype(F32) * (-2.0 * math.log(rope_base) / HEAD))
    angles = place.astype(F32) * frequency
    cosine = jnp.cos(angles)
    sine = jnp.sin(angles) * jnp.where(lane % HEAD < HALF, -1.0, 1.0)

    queries, keys, values = qkv_heads(x_all, qkv_full, cosine, sine)
    attended_heads, lse = attend(queries, keys, values)

    def row_pieces(array):
        return [array[n * positions : (n + 1) * positions] for n in range(seq_size)]

    attended_pieces = exchange_seq(row_pieces(attended_heads))
    attended = jnp.concatenate(attended_pieces, 1)
    attn_out_ordered = jnp.concatenate(
        [
            lax.dynamic_slice(
                attn_out_full, ((me ^ member) * local_width, 0), (local_width, width)
            )
            for member in order
        ],
        0,
    )
    mixed = tokens + dot_nn(attended, attn_out_ordered)
    xhat_mlp, inverse_mlp = centred_stats(mixed)
    x_mlp_all = jnp.concatenate(gather_seq(xhat_mlp.astype(BF16)), 0)
    own_cotangent = cotangent.reshape(positions, width)
    cotangent_all = jnp.concatenate(gather_seq(own_cotangent), 0)

    hidden, gate_up_grad, back, out = mlp(x_mlp_all, cotangent_all, in_full, mlp_out_full)
    back_sum = scatter_seq(row_pieces(back))
    output = (mixed + scatter_seq(row_pieces(out))).astype(BF16).reshape(activations.shape)
    grad_in = dot_tn(x_mlp_all, gate_up_grad).astype(BF16)
    grad_mlp_out = dot_tn(hidden, cotangent_all).astype(BF16)

    mixed_grad = own_cotangent.astype(F32) + norm_backward(back_sum, xhat_mlp, inverse_mlp)
    mixed_low = mixed_grad.astype(BF16)
    attended_grad = dot_nt(mixed_low, attn_out_ordered).astype(BF16)
    grads = jnp.concatenate(
        exchange_seq(
            [attended_grad[:, n * local_width : (n + 1) * local_width] for n in range(seq_size)]
        ),
        0,
    )
    grad_attn_out = dot_tn(jnp.concatenate(by_member(attended_pieces), 1), mixed_low).astype(BF16)
    grad_attn_out = scatter_seq(
        [
            lax.dynamic_slice(grad_attn_out, (0, (me ^ member) * local_width), (width, local_width))
            for member in order
        ]
    ).astype(BF16)

    d_queries, d_keys, d_values = attend_back(
        queries, keys, values, grads, attended_heads, lse, cosine, sine
    )
    packed_grad = jnp.concatenate([d_queries, d_keys, d_values], 1)
    normed_grad = dot_nt(packed_grad, qkv_full).astype(BF16)
    grad_qkv = dot_tn(x_all, packed_grad).astype(BF16)
    normed_grad = scatter_seq(row_pieces(normed_grad))
    d_input = (mixed_grad + norm_backward(normed_grad, xhat, inverse)).astype(BF16)
    d_input = d_input.reshape(activations.shape)

    def reduce_fsdp(values):
        return lax.psum_scatter(values, "fsdp", scatter_dimension=0, tiled=True)

    sum_in = reduce_fsdp(grad_in)
    sum_mlp_out = reduce_fsdp(grad_mlp_out)
    sum_attn_out = reduce_fsdp(grad_attn_out)
    sum_qkv = scatter_fsdp(grad_qkv).astype(BF16)

    in_pieces = [
        piece.reshape(shard, 2 * fsdp_size, unit_share) for piece in by_member(gather_seq(sum_in))
    ]
    all_in = jnp.concatenate(in_pieces, 2)[:, :, :ff_shard].reshape(shard, -1).astype(F32)
    all_mlp_out = jnp.concatenate(by_member(gather_seq(sum_mlp_out)), 0)[:ff_shard].astype(F32)
    all_attn_out = jnp.concatenate(by_member(gather_seq(sum_attn_out)), 1).astype(F32)
    qkv_pieces = by_member(gather_seq(sum_qkv))
    all_qkv = jnp.concatenate(
        [
            piece[:, part * local_width : (part + 1) * local_width]
            for part in range(3)
            for piece in qkv_pieces
        ],
        1,
    ).astype(F32)
    grad_gain_attn = jnp.sum(all_qkv * w_qkv.astype(F32), 1)
    grad_gain_mlp = jnp.sum(all_in * w_in.astype(F32), 1)
    return (
        output,
        d_input,
        grad_gain_attn,
        grad_gain_mlp,
        all_qkv * own_gain_attn,
        all_attn_out,
        all_in * own_gain_mlp,
        all_mlp_out,
    )


def solution(mesh):
    in_specs = (
        P("fsdp", "seq", None),
        P("fsdp", "seq", None),
        P("fsdp"),
        P("fsdp", None),
        P("fsdp", None),
        P("fsdp"),
        P("fsdp", None),
        P("fsdp", None),
    )
    out_specs = (
        P("fsdp", "seq", None),
        P("fsdp", "seq", None),
        P("fsdp"),
        P("fsdp"),
        P("fsdp", None),
        P("fsdp", None),
        P("fsdp", None),
        P("fsdp", None),
    )
    body = functools.partial(local, mesh.shape["seq"], mesh.shape["fsdp"])
    return jax.shard_map(body, mesh=mesh, in_specs=in_specs, out_specs=out_specs, check_vma=False)
```

```python
import functools
import math

import jax
import jax.numpy as jnp
from jax import lax
from jax.experimental import pallas as pl
from jax.experimental.pallas import tpu as pltpu
from jax.sharding import PartitionSpec as P

HEADS = 16
HEAD = 64
HALF = HEAD // 2
ROW_TILE = 16
BF16 = jnp.bfloat16
F32 = jnp.float32

eps = 1e-05
rope_base = 160000.0
VMEM_BYTES = 60 << 20


def dot_nn(a, b):
    return lax.dot_general(a, b, (((1,), (0,)), ((), ())), preferred_element_type=F32)


def dot_nt(a, b):
    return lax.dot_general(a, b, (((1,), (1,)), ((), ())), preferred_element_type=F32)


def dot_tn(a, b):
    return lax.dot_general(a, b, (((0,), (0,)), ((), ())), preferred_element_type=F32)


def block_rows(rows, wanted):
    best = rows
    for size in range(ROW_TILE, min(rows, wanted) + 1, ROW_TILE):
        if rows % size == 0:
            best = size
    return best


def centred_stats(values):
    average = jnp.mean(values, -1, keepdims=True)
    centred = values - average
    inverse = lax.rsqrt(jnp.mean(centred * centred, -1, keepdims=True) + eps)
    return centred * inverse, inverse


def norm_backward(grad, xhat, inverse):
    return inverse * (
        grad
        - jnp.mean(grad, -1, keepdims=True)
        - xhat * jnp.mean(grad * xhat, -1, keepdims=True)
    )


def partner(values):
    width = values.shape[-1]
    if width % 128:
        return jnp.concatenate([values[:, HALF:], values[:, :HALF]], 1)
    lane = lax.broadcasted_iota(jnp.int32, values.shape, 1)
    return jnp.where(
        lane % HEAD < HALF,
        pltpu.roll(values, width - HALF, 1),
        pltpu.roll(values, HALF, 1),
    )


def head_of_lane(shape):
    return lax.broadcasted_iota(jnp.int32, shape, 1) // HEAD


def only_head(values, head):
    return jnp.where(head_of_lane(values.shape) == head, values, jnp.zeros_like(values))


def take_piece(piece_refs, steps, scratch):
    for at, ref in enumerate(piece_refs):

        @pl.when(pl.program_id(0) // steps == at)
        def _(ref=ref):
            scratch[...] = ref[...]

    return scratch[...]


def piece_specs(count, steps, rows, columns):
    return [
        pl.BlockSpec(
            (rows, columns), lambda i, at=at: (jnp.clip(i - at * steps, 0, steps - 1), 0)
        )
        for at in range(count)
    ]


def qkv_body(count, steps, *refs):
    pieces, (w_ref, cos_ref, sin_ref) = refs[:count], refs[count : count + 3]
    q_ref, k_ref, v_ref, x_ref, scratch = refs[-5:]
    width = q_ref.shape[1]
    x = take_piece(pieces, steps, scratch)
    x_ref[...] = x
    packed = dot_nn(x, w_ref[...])
    cosine = cos_ref[...]
    sine = sin_ref[...]
    lanes = cosine.shape[1]
    for group in range(width // lanes):
        here = slice(group * lanes, (group + 1) * lanes)
        for at, ref in enumerate((q_ref, k_ref, v_ref)):
            start = (3 * group + at) * lanes
            part = packed[:, start : start + lanes]
            if at < 2:
                part = part * cosine + partner(part) * sine
            ref[:, here] = part.astype(BF16)


def qkv_heads(pieces, weights, cosine, sine, before):
    count = len(pieces)
    rows, depth = pieces[0].shape
    width = weights.shape[1] // 3
    step = block_rows(rows, 320)
    steps = rows // step
    length, table = cosine.shape
    first = count * steps if before else 0
    by_row = lambda columns: pl.BlockSpec((step, columns), lambda i: (i + first, 0))
    total = count * rows
    return pl.pallas_call(
        functools.partial(qkv_body, count, steps),
        grid=(count * steps,),
        in_specs=piece_specs(count, steps, step, depth)
        + [pl.BlockSpec((depth, 3 * width), lambda i: (0, 0)), by_row(table), by_row(table)]
        + [pl.BlockSpec(memory_space=pl.ANY)] * len(before),
        out_specs=[by_row(width)] * 3 + [by_row(depth)],
        out_shape=[jax.ShapeDtypeStruct((length, width), BF16)] * 3
        + [jax.ShapeDtypeStruct((length, depth), BF16)],
        scratch_shapes=[pltpu.VMEM((step, depth), BF16)],
        input_output_aliases={count + 3 + at: at for at in range(len(before))},
        compiler_params=pltpu.CompilerParams(vmem_limit_bytes=VMEM_BYTES),
        cost_estimate=pl.CostEstimate(
            flops=6 * total * depth * width,
            bytes_accessed=2 * (2 * total * depth + 3 * depth * width + 3 * total * width),
            transcendentals=0,
        ),
        name="qkv_rope",
    )(*pieces, weights, cosine, sine, *before)


def attend_body(q_ref, k_ref, v_ref, out_ref, lse_ref):
    width = q_ref.shape[1]
    queries = q_ref[...] * jnp.asarray(HEAD**-0.5, BF16)
    keys = k_ref[...]
    values = v_ref[...]
    for head in range(width // HEAD):
        scores = dot_nt(only_head(queries, head), keys)
        peak = jnp.max(scores, -1, keepdims=True)
        exponent = jnp.exp(scores - peak)
        total = jnp.sum(exponent, -1, keepdims=True)
        out = dot_nn(exponent.astype(BF16), values) / total
        lse = jnp.broadcast_to(peak + jnp.log(total), out.shape)
        if head:
            here = head_of_lane(out.shape) == head
            out = jnp.where(here, out, previous_out)
            lse = jnp.where(here, lse, previous_lse)
        previous_out, previous_lse = out, lse
    out_ref[...] = out.astype(BF16)
    lse_ref[...] = lse.T


def attend(queries, keys, values, group):
    rows, local_width = queries.shape
    width = min(128, local_width)
    step = block_rows(rows, 256)
    q_spec = pl.BlockSpec((step, width), lambda i: (i, group))
    k_spec = pl.BlockSpec((rows, width), lambda i: (0, group))
    return pl.pallas_call(
        attend_body,
        grid=(rows // step,),
        in_specs=[q_spec, k_spec, k_spec],
        out_specs=[
            pl.BlockSpec((step, width), lambda i: (i, 0)),
            pl.BlockSpec((width, step), lambda i: (0, i)),
        ],
        out_shape=[
            jax.ShapeDtypeStruct((rows, width), BF16),
            jax.ShapeDtypeStruct((width, rows), F32),
        ],
        compiler_params=pltpu.CompilerParams(vmem_limit_bytes=VMEM_BYTES),
        cost_estimate=pl.CostEstimate(
            flops=16 * rows * rows * width,
            bytes_accessed=8 * rows * width,
            transcendentals=rows * rows * width // HEAD,
        ),
        name="attend",
    )(queries, keys, values)


def attend_back_body(
    q_ref, k_ref, v_ref, g_ref, out_ref, lse_ref, cos_ref, sin_ref, packed_ref, dk_sum, dv_sum
):
    step_rows, width = q_ref.shape
    step = pl.program_id(0)

    @pl.when(step == 0)
    def _():
        dk_sum[...] = jnp.zeros_like(dk_sum)
        dv_sum[...] = jnp.zeros_like(dv_sum)

    factor = HEAD**-0.5
    queries = q_ref[...] * jnp.asarray(factor, BF16)
    keys = k_ref[...]
    values = v_ref[...]
    grads = g_ref[...]
    product = (grads.astype(F32) * out_ref[...].astype(F32)).T
    dq = jnp.zeros(product.shape, F32)
    for head in range(width // HEAD):
        own_queries = only_head(queries, head)
        own_grads = only_head(grads, head)
        lse = lse_ref[head * HEAD : head * HEAD + 1, :]
        inner = jnp.sum(product[head * HEAD : (head + 1) * HEAD], 0, keepdims=True)
        probs = jnp.exp(dot_nt(keys, own_queries) - lse)
        prob_grad = dot_nt(values, own_grads)
        score_grad = (probs * (prob_grad - inner)).astype(BF16)
        dv_sum[...] += dot_nn(probs.astype(BF16), own_grads)
        dk_sum[...] += dot_nn(score_grad, own_queries)
        dq = dq + dot_tn(only_head(keys, head), score_grad)
    dq = (dq.T * factor).astype(BF16).astype(F32)
    here = pl.ds(pl.multiple_of(step * step_rows, ROW_TILE), step_rows)
    packed_ref[here, :width] = (dq * cos_ref[here, :] - partner(dq) * sin_ref[here, :]).astype(BF16)

    @pl.when(step == pl.num_programs(0) - 1)
    def _():
        dk = dk_sum[...].astype(BF16).astype(F32)
        packed_ref[:, width : 2 * width] = (
            dk * cos_ref[...] - partner(dk) * sin_ref[...]
        ).astype(BF16)
        packed_ref[:, 2 * width :] = dv_sum[...].astype(BF16)


def attend_back(queries, keys, values, grads, out, lse, cosine, sine, group):
    rows, local_width = queries.shape
    width = min(128, local_width)
    step = block_rows(rows, 512)
    q_spec = pl.BlockSpec((step, width), lambda i: (i, group))
    k_spec = pl.BlockSpec((rows, width), lambda i: (0, group))
    own_spec = pl.BlockSpec((step, width), lambda i: (i, 0))
    all_spec = pl.BlockSpec((rows, width), lambda i: (0, 0))
    return pl.pallas_call(
        attend_back_body,
        grid=(rows // step,),
        in_specs=[
            q_spec, k_spec, k_spec, own_spec, own_spec,
            pl.BlockSpec((width, step), lambda i: (0, i)),
            all_spec, all_spec,
        ],
        out_specs=pl.BlockSpec((rows, 3 * width), lambda i: (0, 0)),
        out_shape=jax.ShapeDtypeStruct((rows, 3 * width), BF16),
        scratch_shapes=[pltpu.VMEM((rows, width), F32)] * 2,
        compiler_params=pltpu.CompilerParams(vmem_limit_bytes=VMEM_BYTES),
        cost_estimate=pl.CostEstimate(
            flops=40 * rows * rows * width,
            bytes_accessed=20 * rows * width,
            transcendentals=rows * rows * width // HEAD,
        ),
        name="attend_back",
    )(queries, keys, values, grads, out, lse, cosine, sine)


def mlp_body(count, steps, *refs):
    x_pieces, c_pieces = refs[:count], refs[count : 2 * count]
    wi_ref, wo_ref = refs[2 * count : 2 * count + 2]
    x_scratch, c_scratch = refs[-2:]
    results = refs[-2 - 4 - 2 * count : -2]
    hidden_ref, gate_up_ref, x_ref, c_ref = results[:4]
    back_refs, out_refs = results[4 : 4 + count], results[4 + count :]
    units = wo_ref.shape[0]
    x = take_piece(x_pieces, steps, x_scratch)
    cotangent = take_piece(c_pieces, steps, c_scratch)
    x_ref[...] = x
    c_ref[...] = cotangent
    gate_up = dot_nn(x, wi_ref[...])
    hidden_grad = dot_nt(cotangent, wo_ref[...])
    gate = gate_up[:, :units]
    up = gate_up[:, units:]
    share = 0.5 * (1.0 + lax.erf(gate * 2.0**-0.5))
    activated = gate * share
    slope = share + gate * jnp.exp(-0.5 * gate * gate) * (2.0 * math.pi) ** -0.5
    hidden = (activated * up).astype(BF16)
    hidden_ref[...] = hidden
    gate_grad = (hidden_grad * up * slope).astype(BF16)
    up_grad = (hidden_grad * activated).astype(BF16)
    both = jnp.concatenate([gate_grad, up_grad], 1)
    gate_up_ref[...] = both
    back = dot_nt(both, wi_ref[...]).astype(BF16)
    out = dot_nn(hidden, wo_ref[...]).astype(BF16)
    for at in range(count):

        @pl.when(pl.program_id(0) // steps == at)
        def _(at=at):
            back_refs[at][...] = back
            out_refs[at][...] = out


def mlp(x_pieces, c_pieces, w_in, w_out, length, before):
    count = len(x_pieces)
    rows, depth = x_pieces[0].shape
    units = w_out.shape[0]
    step = block_rows(rows, 320)
    steps = rows // step
    total = count * rows
    first = count * steps if before else 0
    by_row = lambda columns: pl.BlockSpec((step, columns), lambda i: (i + first, 0))
    whole = lambda shape: pl.BlockSpec(shape, lambda i: (0, 0))
    pieces = piece_specs(count, steps, step, depth)
    results = pl.pallas_call(
        functools.partial(mlp_body, count, steps),
        grid=(count * steps,),
        in_specs=pieces
        + pieces
        + [whole((depth, 2 * units)), whole(w_out.shape)]
        + [pl.BlockSpec(memory_space=pl.ANY)] * len(before),
        out_specs=[by_row(units), by_row(2 * units), by_row(depth), by_row(depth)]
        + pieces
        + pieces,
        out_shape=[
            jax.ShapeDtypeStruct((length, columns), BF16)
            for columns in (units, 2 * units, depth, depth)
        ]
        + [jax.ShapeDtypeStruct((rows, depth), BF16)] * (2 * count),
        scratch_shapes=[pltpu.VMEM((step, depth), BF16)] * 2,
        input_output_aliases={2 * count + 2 + at: at for at in range(len(before))},
        compiler_params=pltpu.CompilerParams(vmem_limit_bytes=VMEM_BYTES),
        cost_estimate=pl.CostEstimate(
            flops=12 * total * depth * units,
            bytes_accessed=2 * total * (6 * depth + 3 * units) + 6 * depth * units,
            transcendentals=2 * total * units,
        ),
        name="mlp",
    )(*x_pieces, *c_pieces, w_in, w_out, *before)
    return results[:4], results[4 : 4 + count], results[4 + count :]


def token_grad_body(groups, count, steps, *refs):
    packed = jnp.concatenate([ref[...] for ref in refs[:groups]], 1)
    results = refs[groups + 1 :]
    grad = dot_nt(packed, refs[groups][...]).astype(BF16)
    for at in range(count):

        @pl.when(pl.program_id(0) // steps == at)
        def _(at=at):
            results[at][...] = grad


def token_grad(packed, weights, count, positions, first):
    groups = len(packed)
    depth, columns = weights.shape
    step = block_rows(positions, 320)
    steps = positions // step
    total = count * positions
    return pl.pallas_call(
        functools.partial(token_grad_body, groups, count, steps),
        grid=(count * steps,),
        in_specs=[
            pl.BlockSpec((step, columns // groups), lambda i: (i + first * steps, 0))
        ] * groups
        + [pl.BlockSpec((depth, columns), lambda i: (0, 0))],
        out_specs=piece_specs(count, steps, step, depth),
        out_shape=[jax.ShapeDtypeStruct((positions, depth), BF16)] * count,
        compiler_params=pltpu.CompilerParams(vmem_limit_bytes=VMEM_BYTES),
        cost_estimate=pl.CostEstimate(
            flops=2 * total * depth * columns,
            bytes_accessed=2 * (total * depth + depth * columns + total * columns),
            transcendentals=0,
        ),
        name="token_grad",
    )(*packed, weights)


def local(seq_size, fsdp_size, activations, cotangent, gain_attn, w_qkv, w_attn_out, gain_mlp, w_in, w_mlp_out):
    _, positions, width = activations.shape
    shard = w_qkv.shape[0]
    ff_shard = w_mlp_out.shape[0]
    local_width = width // seq_size
    length = positions * seq_size
    half = seq_size // 2
    lanes = min(128, local_width)
    groups = local_width // lanes
    me = lax.axis_index("seq")
    row = lax.axis_index("fsdp")
    after = lax.optimization_barrier


    def swap(values, axis, size, offset):
        return lax.ppermute(values, axis, [(i, i ^ offset) for i in range(size)])

    def swap_seq(values, offset):
        return swap(values, "seq", seq_size, offset)

    def spread(values):
        pieces = [values]
        bit = 1
        while bit < half:
            pieces = pieces + [swap_seq(piece, bit) for piece in pieces]
            bit *= 2
        return pieces

    def gather_seq(values):
        return spread(values) + spread(swap_seq(values, half))

    def fold(pieces):
        pieces = list(pieces)
        while len(pieces) > 1:
            left = len(pieces) // 2
            got = [swap_seq(piece.astype(BF16), left) for piece in pieces[left:]]
            pieces = [kept.astype(F32) + other.astype(F32) for kept, other in zip(pieces, got)]
        return pieces[0].astype(F32)

    def far_sum(pieces):
        return swap_seq(fold(pieces).astype(BF16), half)

    def exchange_seq(pieces):
        return [pieces[0]] + [swap_seq(pieces[k], k) for k in range(1, seq_size)]

    def by_member(pieces):
        stacked = jnp.stack(pieces)
        return [
            lax.dynamic_index_in_dim(stacked, me ^ member, 0, keepdims=False)
            for member in range(seq_size)
        ]

    def gather_fsdp(values):
        rows = values.shape[0]
        gathered = values
        at = 0
        bit = fsdp_size // 2
        while bit:
            other = swap(gathered, "fsdp", fsdp_size, bit)
            high = (row & bit) != 0
            gathered = jnp.stack(
                [jnp.where(high, other, gathered), jnp.where(high, gathered, other)], at
            )
            at += 1
            bit //= 2
        return gathered.reshape(fsdp_size * rows, values.shape[1])

    def halve_fsdp(values, bit):
        rows = shard
        blocks = values.shape[0] // rows
        left = values.reshape(blocks // 2, 2, rows, values.shape[1])
        mine = jnp.where((row & bit) != 0, 1, 0)
        kept = lax.dynamic_index_in_dim(left, mine, 1, keepdims=False)
        sent = lax.dynamic_index_in_dim(left, 1 - mine, 1, keepdims=False)
        total = kept.astype(F32) + swap(sent, "fsdp", fsdp_size, bit).astype(F32)
        return total.astype(BF16).reshape(blocks // 2 * rows, values.shape[1])

    def reduce_fsdp(values):
        return lax.psum_scatter(values, "fsdp", scatter_dimension=0, tiled=True)

    own_gain_attn = gain_attn.astype(F32)[:, None]
    own_gain_mlp = gain_mlp.astype(F32)[:, None]

    qkv_slice = jnp.concatenate(
        [
            lax.dynamic_slice(
                w_qkv, (0, part * width + me * local_width + group * lanes), (shard, lanes)
            )
            for group in range(groups)
            for part in range(3)
        ],
        1,
    )
    qkv_slice = (qkv_slice.astype(F32) * own_gain_attn).astype(BF16)
    qkv_full = gather_fsdp(qkv_slice)

    tokens = activations.reshape(positions, width).astype(F32)
    xhat, inverse = centred_stats(tokens)
    own_x = xhat.astype(BF16)
    far_x = swap_seq(own_x, half)
    near_x_pieces = spread(own_x)
    far_x_pieces = spread(far_x)
    own_cotangent = cotangent.reshape(positions, width)
    near_c_pieces = spread(own_cotangent)
    far_c_pieces = spread(swap_seq(after((own_cotangent, far_x))[0], half))

    unit_share = -(-ff_shard // seq_size)
    unit_share = -(-unit_share // ROW_TILE) * ROW_TILE
    padding = unit_share * seq_size - ff_shard
    units = fsdp_size * unit_share
    attn_out_slice = lax.dynamic_slice(w_attn_out, (0, me * local_width), (shard, local_width))
    mlp_out_slice = lax.dynamic_slice(
        jnp.pad(w_mlp_out, ((0, padding), (0, 0))), (me * unit_share, 0), (unit_share, width)
    )
    in_slice = jnp.pad(
        w_in.reshape(shard, 2 * fsdp_size, ff_shard), ((0, 0), (0, 0), (0, padding))
    )
    in_slice = lax.dynamic_slice(
        in_slice, (0, 0, me * unit_share), (shard, 2 * fsdp_size, unit_share)
    ).reshape(shard, 2 * units)
    in_slice = (in_slice.astype(F32) * own_gain_mlp).astype(BF16)
    rows = math.gcd(unit_share, shard)
    tall, wide = unit_share // rows, shard // rows
    mlp_out_slice = (
        mlp_out_slice.reshape(tall, rows, wide, width // wide)
        .transpose(2, 1, 0, 3)
        .reshape(shard, tall * width // wide)
    )
    later = lax.all_gather(
        jnp.concatenate([in_slice, mlp_out_slice, attn_out_slice], 1), "fsdp", axis=0, tiled=True
    )
    mlp_out_full = (
        later[:, 2 * units : 2 * units + tall * width // wide]
        .reshape(fsdp_size, wide, rows, tall, width // wide)
        .transpose(0, 3, 2, 1, 4)
        .reshape(units, width)
    )
    lane = lax.broadcasted_iota(jnp.int32, (length, lanes), 1)
    at = lax.broadcasted_iota(jnp.int32, (length, lanes), 0)
    place = ((at // positions) ^ me) * positions + at % positions
    frequency = jnp.exp((lane % HALF).astype(F32) * (-2.0 * math.log(rope_base) / HEAD))
    angles = place.astype(F32) * frequency
    cosine = jnp.cos(angles)
    sine = jnp.sin(angles) * jnp.where(lane % HEAD < HALF, -1.0, 1.0)

    begun = qkv_heads(near_x_pieces, qkv_full, cosine, sine, [])
    queries, keys, values, x_all = qkv_heads(far_x_pieces, qkv_full, cosine, sine, begun)

    def row_pieces(array):
        return [array[k * positions : (k + 1) * positions] for k in range(seq_size)]

    heads = [attend(queries, keys, values, 0)]
    group_pieces = [exchange_seq(row_pieces(heads[0][0]))]
    sections = gather_seq(after((later, heads[0][0]))[0][:, -local_width:])
    attn_out_full = jnp.concatenate(by_member(sections), 1)
    for group in range(1, groups):
        heads.append(attend(after((queries, later))[0], keys, values, group))
        group_pieces.append(exchange_seq(row_pieces(heads[group][0])))
    attended_pieces = [jnp.concatenate(pieces, 1) for pieces in zip(*group_pieces)]
    attn_out_ordered = jnp.concatenate(
        [
            lax.dynamic_slice(
                attn_out_full, ((me ^ member) * local_width, 0), (local_width, width)
            )
            for member in range(seq_size)
        ],
        0,
    )
    attended = jnp.concatenate(attended_pieces, 1)
    mixed = tokens + dot_nn(attended, attn_out_ordered)
    xhat_mlp, inverse_mlp = centred_stats(mixed)
    own_x_mlp = xhat_mlp.astype(BF16)
    far_x_mlp_pieces = spread(swap_seq(own_x_mlp, half))
    begun, near_back, near_out = mlp(
        spread(own_x_mlp), near_c_pieces, later, mlp_out_full, length, []
    )
    (hidden, gate_up_grad, x_mlp_all, cotangent_all), far_back, far_out = mlp(
        far_x_mlp_pieces, far_c_pieces, later, mlp_out_full, length, begun
    )
    back_far = far_sum(far_back)
    back_near = fold(near_back)
    grad_mlp_out = dot_tn(hidden, cotangent_all).astype(BF16)
    grad_in = dot_tn(x_mlp_all, gate_up_grad).astype(BF16)
    back_far, grad_mlp_out, grad_in = after((back_far, grad_mlp_out, grad_in))

    mixed_grad = own_cotangent.astype(F32) + norm_backward(
        back_near + back_far.astype(F32), xhat_mlp, inverse_mlp
    )
    mixed_low = mixed_grad.astype(BF16)
    attended_grad = dot_nt(mixed_low, attn_out_ordered).astype(BF16)
    grads = []
    for group in range(groups):
        columns = [k * local_width + group * lanes for k in range(seq_size)]
        pieces = [attended_grad[:, start : start + lanes] for start in columns]
        grads.append(jnp.concatenate(exchange_seq(pieces), 0))
    grad_attn_out = dot_tn(jnp.concatenate(by_member(attended_pieces), 1), mixed_low).astype(BF16)
    grads[0], grad_attn_out = after((grads[0], grad_attn_out))
    column_pieces = [
        lax.dynamic_slice(grad_attn_out, (0, (me ^ k) * local_width), (width, local_width))
        for k in range(seq_size)
    ]
    near_attn_out = fold(column_pieces[:half])
    far_attn_out = fold(column_pieces[half:]).astype(BF16)
    sum_near_out = fold(near_out)
    sum_far_out = fold(far_out).astype(BF16)
    grads[0], sum_far_out, far_attn_out = after((grads[0], sum_far_out, far_attn_out))
    sum_far_out = swap_seq(sum_far_out, half)
    far_attn_out = swap_seq(far_attn_out, half)

    def back_of(group):
        out, lse = heads[group]
        return attend_back(queries, keys, values, grads[group], out, lse, cosine, sine, group)

    packed = [back_of(0)]
    packed[0], sum_far_out, far_attn_out = after((packed[0], sum_far_out, far_attn_out))
    output = (mixed + (sum_near_out + sum_far_out.astype(F32))).astype(BF16)
    grad_attn_out = (near_attn_out + far_attn_out.astype(F32)).astype(BF16)
    first_grads = jnp.concatenate(
        [dot_tn(x_all, packed[0]).astype(BF16), grad_attn_out], 1
    )
    sum_in = reduce_fsdp(grad_in)
    sum_mlp_out = reduce_fsdp(after((grad_mlp_out, grad_in))[0])
    reduced = [halve_fsdp(first_grads, 1)]
    for group in range(1, groups):
        grads[group], output, first_grads, sum_in = after(
            (grads[group], output, first_grads, sum_in)
        )
        packed.append(back_of(group))

    far_grads = token_grad(packed, qkv_full, half, positions, half)
    far_grads = fold(far_grads).astype(BF16)
    near_grads = token_grad(packed, qkv_full, half, positions, 0)
    if groups > 1:
        last_grads = [dot_tn(x_all, section).astype(BF16) for section in packed[1:]]
        last_grads, far_grads = after((last_grads, far_grads))
        reduced += [halve_fsdp(section, 1) for section in last_grads]
    reduced[-1], sum_mlp_out = after((reduced[-1], sum_mlp_out))
    far_grads = swap_seq(far_grads, half)
    normed_grad = far_grads.astype(F32) + fold(near_grads)
    d_input = (mixed_grad + norm_backward(normed_grad, xhat, inverse)).astype(BF16)
    reduced = jnp.concatenate(reduced, 1)
    bit = 2
    while bit < fsdp_size:
        reduced = halve_fsdp(reduced, bit)
        bit *= 2

    in_pieces = by_member(gather_seq(sum_in))
    all_in = jnp.concatenate(
        [piece.reshape(shard, 2 * fsdp_size, unit_share) for piece in in_pieces], 2
    )
    all_in = all_in[:, :, :ff_shard].reshape(shard, -1).astype(F32)
    all_mlp_out = jnp.concatenate(by_member(gather_seq(sum_mlp_out)), 0)[:ff_shard].astype(F32)
    pieces = by_member(gather_seq(reduced))
    section = 3 * lanes
    all_attn_out = jnp.concatenate(
        [piece[:, section : section + local_width] for piece in pieces], 1
    ).astype(F32)
    starts = [0] + [section * group + local_width for group in range(1, groups)]
    all_qkv = jnp.concatenate(
        [
            piece[:, start + part * lanes : start + (part + 1) * lanes]
            for part in range(3)
            for piece in pieces
            for start in starts
        ],
        1,
    ).astype(F32)
    grad_gain_attn = jnp.sum(all_qkv * w_qkv.astype(F32), 1)
    grad_gain_mlp = jnp.sum(all_in * w_in.astype(F32), 1)
    return (
        output.reshape(activations.shape),
        d_input.reshape(activations.shape),
        grad_gain_attn,
        grad_gain_mlp,
        all_qkv * own_gain_attn,
        all_attn_out,
        all_in * own_gain_mlp,
        all_mlp_out,
    )


def solution(mesh):
    in_specs = (
        P("fsdp", "seq", None),
        P("fsdp", "seq", None),
        P("fsdp"),
        P("fsdp", None),
        P("fsdp", None),
        P("fsdp"),
        P("fsdp", None),
        P("fsdp", None),
    )
    out_specs = (
        P("fsdp", "seq", None),
        P("fsdp", "seq", None),
        P("fsdp"),
        P("fsdp"),
        P("fsdp", None),
        P("fsdp", None),
        P("fsdp", None),
        P("fsdp", None),
    )
    body = functools.partial(local, mesh.shape["seq"], mesh.shape["fsdp"])
    return jax.shard_map(body, mesh=mesh, in_specs=in_specs, out_specs=out_specs, check_vma=False)
```

```python
import functools
import math

import jax
import jax.numpy as jnp
from jax import lax
from jax.experimental import pallas as pl
from jax.experimental.pallas import tpu as pltpu
from jax.sharding import PartitionSpec as P

HEADS = 16
HEAD = 64
HALF = HEAD // 2
ROW_TILE = 16
BF16 = jnp.bfloat16
F32 = jnp.float32

eps = 1e-05
rope_base = 160000.0
VMEM_BYTES = 60 << 20


def dot_nn(a, b):
    return lax.dot_general(a, b, (((1,), (0,)), ((), ())), preferred_element_type=F32)


def dot_nt(a, b):
    return lax.dot_general(a, b, (((1,), (1,)), ((), ())), preferred_element_type=F32)


def dot_tn(a, b):
    return lax.dot_general(a, b, (((0,), (0,)), ((), ())), preferred_element_type=F32)


def block_rows(rows, wanted):
    best = rows
    for size in range(ROW_TILE, min(rows, wanted) + 1, ROW_TILE):
        if rows % size == 0:
            best = size
    return best


def centred_stats(values):
    average = jnp.mean(values, -1, keepdims=True)
    centred = values - average
    inverse = lax.rsqrt(jnp.mean(centred * centred, -1, keepdims=True) + eps)
    return centred * inverse, inverse


def norm_backward(grad, xhat, inverse):
    return inverse * (
        grad
        - jnp.mean(grad, -1, keepdims=True)
        - xhat * jnp.mean(grad * xhat, -1, keepdims=True)
    )


def partner(values):
    width = values.shape[-1]
    if width % 128:
        return jnp.concatenate([values[:, HALF:], values[:, :HALF]], 1)
    lane = lax.broadcasted_iota(jnp.int32, values.shape, 1)
    return jnp.where(
        lane % HEAD < HALF,
        pltpu.roll(values, width - HALF, 1),
        pltpu.roll(values, HALF, 1),
    )


def head_of_lane(shape):
    return lax.broadcasted_iota(jnp.int32, shape, 1) // HEAD


def only_head(values, head):
    return jnp.where(head_of_lane(values.shape) == head, values, jnp.zeros_like(values))


def take_piece(piece_refs, steps, scratch):
    for at, ref in enumerate(piece_refs):

        @pl.when(pl.program_id(0) // steps == at)
        def _(ref=ref):
            scratch[...] = ref[...]

    return scratch[...]


def piece_specs(count, steps, rows, columns):
    return [
        pl.BlockSpec(
            (rows, columns), lambda i, at=at: (jnp.clip(i - at * steps, 0, steps - 1), 0)
        )
        for at in range(count)
    ]


def bit_reversed(count):
    order = [0]
    while len(order) < count:
        order = [2 * at for at in order] + [2 * at + 1 for at in order]
    return order


def reorder(values, blocks):
    size = values.shape[1] // blocks
    return jnp.concatenate(
        [values[:, at * size : (at + 1) * size] for at in bit_reversed(blocks)], 1
    )


def qkv_body(blocks, count, steps, *refs):
    pieces, (w_ref, cos_ref, sin_ref) = refs[:count], refs[count : count + 3]
    q_ref, k_ref, v_ref, x_ref, scratch = refs[-5:]
    width = q_ref.shape[1]
    x = reorder(take_piece(pieces, steps, scratch), blocks)
    x_ref[...] = x
    packed = dot_nn(x, w_ref[:, : 3 * q_ref.shape[1]])
    cosine = cos_ref[...]
    sine = sin_ref[...]
    lanes = cosine.shape[1]
    for group in range(width // lanes):
        here = slice(group * lanes, (group + 1) * lanes)
        for at, ref in enumerate((q_ref, k_ref, v_ref)):
            start = (3 * group + at) * lanes
            part = packed[:, start : start + lanes]
            if at < 2:
                part = part * cosine + partner(part) * sine
            ref[:, here] = part.astype(BF16)


def qkv_heads(pieces, weights, cosine, sine, blocks, before):
    count = len(pieces)
    rows, depth = pieces[0].shape
    width = weights.shape[1] // 4
    step = block_rows(rows, 320)
    steps = rows // step
    length, table = cosine.shape
    first = count * steps if before else 0
    by_row = lambda columns: pl.BlockSpec((step, columns), lambda i: (i + first, 0))
    total = count * rows
    return pl.pallas_call(
        functools.partial(qkv_body, blocks, count, steps),
        grid=(count * steps,),
        in_specs=piece_specs(count, steps, step, depth)
        + [pl.BlockSpec(weights.shape, lambda i: (0, 0)), by_row(table), by_row(table)]
        + [pl.BlockSpec(memory_space=pl.ANY)] * len(before),
        out_specs=[by_row(width)] * 3 + [by_row(depth)],
        out_shape=[jax.ShapeDtypeStruct((length, width), BF16)] * 3
        + [jax.ShapeDtypeStruct((length, depth), BF16)],
        scratch_shapes=[pltpu.VMEM((step, depth), BF16)],
        input_output_aliases={count + 3 + at: at for at in range(len(before))},
        compiler_params=pltpu.CompilerParams(vmem_limit_bytes=VMEM_BYTES),
        cost_estimate=pl.CostEstimate(
            flops=6 * total * depth * width,
            bytes_accessed=2 * (2 * total * depth + 3 * depth * width + 3 * total * width),
            transcendentals=0,
        ),
        name="qkv_rope",
    )(*pieces, weights, cosine, sine, *before)


def attend_body(q_ref, k_ref, v_ref, out_ref, lse_ref):
    width = q_ref.shape[1]
    queries = q_ref[...] * jnp.asarray(HEAD**-0.5, BF16)
    keys = k_ref[...]
    values = v_ref[...]
    for head in range(width // HEAD):
        scores = dot_nt(only_head(queries, head), keys)
        peak = jnp.max(scores, -1, keepdims=True)
        exponent = jnp.exp(scores - peak)
        total = jnp.sum(exponent, -1, keepdims=True)
        out = dot_nn(exponent.astype(BF16), values) / total
        lse = jnp.broadcast_to(peak + jnp.log(total), out.shape)
        if head:
            here = head_of_lane(out.shape) == head
            out = jnp.where(here, out, previous_out)
            lse = jnp.where(here, lse, previous_lse)
        previous_out, previous_lse = out, lse
    out_ref[...] = out.astype(BF16)
    lse_ref[...] = lse.T


def attend(queries, keys, values, group):
    rows, local_width = queries.shape
    width = min(128, local_width)
    step = block_rows(rows, 256)
    q_spec = pl.BlockSpec((step, width), lambda i: (i, group))
    k_spec = pl.BlockSpec((rows, width), lambda i: (0, group))
    return pl.pallas_call(
        attend_body,
        grid=(rows // step,),
        in_specs=[q_spec, k_spec, k_spec],
        out_specs=[
            pl.BlockSpec((step, width), lambda i: (i, 0)),
            pl.BlockSpec((width, step), lambda i: (0, i)),
        ],
        out_shape=[
            jax.ShapeDtypeStruct((rows, width), BF16),
            jax.ShapeDtypeStruct((width, rows), F32),
        ],
        compiler_params=pltpu.CompilerParams(vmem_limit_bytes=VMEM_BYTES),
        cost_estimate=pl.CostEstimate(
            flops=16 * rows * rows * width,
            bytes_accessed=8 * rows * width,
            transcendentals=rows * rows * width // HEAD,
        ),
        name="attend",
    )(queries, keys, values)


def attend_back_body(
    q_ref, k_ref, v_ref, g_ref, out_ref, lse_ref, cos_ref, sin_ref, packed_ref, dk_sum, dv_sum
):
    step_rows, width = q_ref.shape
    step = pl.program_id(0)

    @pl.when(step == 0)
    def _():
        dk_sum[...] = jnp.zeros_like(dk_sum)
        dv_sum[...] = jnp.zeros_like(dv_sum)

    factor = HEAD**-0.5
    queries = q_ref[...] * jnp.asarray(factor, BF16)
    keys = k_ref[...]
    values = v_ref[...]
    grads = g_ref[...]
    product = (grads.astype(F32) * out_ref[...].astype(F32)).T
    dq = jnp.zeros(product.shape, F32)
    for head in range(width // HEAD):
        own_queries = only_head(queries, head)
        own_grads = only_head(grads, head)
        lse = lse_ref[head * HEAD : head * HEAD + 1, :]
        inner = jnp.sum(product[head * HEAD : (head + 1) * HEAD], 0, keepdims=True)
        probs = jnp.exp(dot_nt(keys, own_queries) - lse)
        prob_grad = dot_nt(values, own_grads)
        score_grad = (probs * (prob_grad - inner)).astype(BF16)
        dv_sum[...] += dot_nn(probs.astype(BF16), own_grads)
        dk_sum[...] += dot_nn(score_grad, own_queries)
        dq = dq + dot_tn(only_head(keys, head), score_grad)
    dq = (dq.T * factor).astype(BF16).astype(F32)
    here = pl.ds(pl.multiple_of(step * step_rows, ROW_TILE), step_rows)
    packed_ref[here, :width] = (dq * cos_ref[here, :] - partner(dq) * sin_ref[here, :]).astype(BF16)

    @pl.when(step == pl.num_programs(0) - 1)
    def _():
        dk = dk_sum[...].astype(BF16).astype(F32)
        packed_ref[:, width : 2 * width] = (
            dk * cos_ref[...] - partner(dk) * sin_ref[...]
        ).astype(BF16)
        packed_ref[:, 2 * width :] = dv_sum[...].astype(BF16)


def attend_back(queries, keys, values, grads, out, lse, cosine, sine, group):
    rows, local_width = queries.shape
    width = min(128, local_width)
    step = block_rows(rows, 512)
    q_spec = pl.BlockSpec((step, width), lambda i: (i, group))
    k_spec = pl.BlockSpec((rows, width), lambda i: (0, group))
    own_spec = pl.BlockSpec((step, width), lambda i: (i, 0))
    all_spec = pl.BlockSpec((rows, width), lambda i: (0, 0))
    return pl.pallas_call(
        attend_back_body,
        grid=(rows // step,),
        in_specs=[
            q_spec, k_spec, k_spec, own_spec, own_spec,
            pl.BlockSpec((width, step), lambda i: (0, i)),
            all_spec, all_spec,
        ],
        out_specs=pl.BlockSpec((rows, 3 * width), lambda i: (0, 0)),
        out_shape=jax.ShapeDtypeStruct((rows, 3 * width), BF16),
        scratch_shapes=[pltpu.VMEM((rows, width), F32)] * 2,
        compiler_params=pltpu.CompilerParams(vmem_limit_bytes=VMEM_BYTES),
        cost_estimate=pl.CostEstimate(
            flops=40 * rows * rows * width,
            bytes_accessed=20 * rows * width,
            transcendentals=rows * rows * width // HEAD,
        ),
        name="attend_back",
    )(queries, keys, values, grads, out, lse, cosine, sine)


def mlp_body(count, steps, blocks, units, *refs):
    x_pieces, c_pieces = refs[:count], refs[count : 2 * count]
    weights_ref = refs[2 * count]
    x_scratch, c_scratch, wo_ref = refs[-3:]
    results = refs[-3 - 4 - 2 * count : -3]
    wi_ref = weights_ref.at[:, : 2 * units]
    depth = wo_ref.shape[1]

    @pl.when(pl.program_id(0) == 0)
    def _():
        shard, share = depth // blocks, units // blocks
        rows = math.gcd(share, shard)
        wide = depth * rows // shard
        for block in range(blocks):
            for tall in range(share // rows):
                for at in range(shard // rows):
                    wo_ref[
                        pl.ds(block * share + tall * rows, rows), at * wide : (at + 1) * wide
                    ] = weights_ref[
                        pl.ds(block * shard + at * rows, rows),
                        2 * units + tall * wide : 2 * units + (tall + 1) * wide,
                    ]

    hidden_ref, gate_up_ref, x_ref, c_ref = results[:4]
    back_refs, out_refs = results[4 : 4 + count], results[4 + count :]
    x = take_piece(x_pieces, steps, x_scratch)
    cotangent = take_piece(c_pieces, steps, c_scratch)
    x_ref[...] = x
    c_ref[...] = cotangent
    gate_up = dot_nn(x, wi_ref[...])
    hidden_grad = dot_nt(cotangent, wo_ref[...])
    gate = gate_up[:, :units]
    up = gate_up[:, units:]
    share = 0.5 * (1.0 + lax.erf(gate * 2.0**-0.5))
    activated = gate * share
    slope = share + gate * jnp.exp(-0.5 * gate * gate) * (2.0 * math.pi) ** -0.5
    hidden = (activated * up).astype(BF16)
    hidden_ref[...] = hidden
    gate_grad = (hidden_grad * up * slope).astype(BF16)
    up_grad = (hidden_grad * activated).astype(BF16)
    both = jnp.concatenate([gate_grad, up_grad], 1)
    gate_up_ref[...] = both
    back = dot_nt(both, wi_ref[...]).astype(BF16)
    out = dot_nn(hidden, wo_ref[...]).astype(BF16)
    for at in range(count):

        @pl.when(pl.program_id(0) // steps == at)
        def _(at=at):
            back_refs[at][...] = back
            out_refs[at][...] = out


def fold_rows(values, shard):
    share, depth = values.shape
    rows = math.gcd(share, shard)
    tall, wide = share // rows, shard // rows
    return (
        values.reshape(tall, rows, wide, depth // wide)
        .transpose(2, 1, 0, 3)
        .reshape(shard, tall * depth // wide)
    )


def mlp(x_pieces, c_pieces, weights, units, blocks, length, before):
    count = len(x_pieces)
    rows, depth = x_pieces[0].shape
    step = block_rows(rows, 320)
    steps = rows // step
    total = count * rows
    first = count * steps if before else 0
    by_row = lambda columns: pl.BlockSpec((step, columns), lambda i: (i + first, 0))
    whole = lambda shape: pl.BlockSpec(shape, lambda i: (0, 0))
    pieces = piece_specs(count, steps, step, depth)
    results = pl.pallas_call(
        functools.partial(mlp_body, count, steps, blocks, units),
        grid=(count * steps,),
        in_specs=pieces
        + pieces
        + [whole(weights.shape)]
        + [pl.BlockSpec(memory_space=pl.ANY)] * len(before),
        out_specs=[by_row(units), by_row(2 * units), by_row(depth), by_row(depth)]
        + pieces
        + pieces,
        out_shape=[
            jax.ShapeDtypeStruct((length, columns), BF16)
            for columns in (units, 2 * units, depth, depth)
        ]
        + [jax.ShapeDtypeStruct((rows, depth), BF16)] * (2 * count),
        scratch_shapes=[pltpu.VMEM((step, depth), BF16)] * 2 + [pltpu.VMEM((units, depth), BF16)],
        input_output_aliases={2 * count + 1 + at: at for at in range(len(before))},
        compiler_params=pltpu.CompilerParams(vmem_limit_bytes=VMEM_BYTES),
        cost_estimate=pl.CostEstimate(
            flops=12 * total * depth * units,
            bytes_accessed=2 * total * (6 * depth + 3 * units) + 6 * depth * units,
            transcendentals=2 * total * units,
        ),
        name="mlp",
    )(*x_pieces, *c_pieces, weights, *before)
    return results[:4], results[4 : 4 + count], results[4 + count :]


def token_grad_body(blocks, groups, count, steps, *refs):
    packed = jnp.concatenate([ref[...] for ref in refs[:groups]], 1)
    results = refs[groups + 1 :]
    weights = refs[groups][:, : packed.shape[1]]
    grad = reorder(dot_nt(packed, weights).astype(BF16), blocks)
    for at in range(count):

        @pl.when(pl.program_id(0) // steps == at)
        def _(at=at):
            results[at][...] = grad


def token_grad(packed, weights, blocks, count, positions, first):
    groups = len(packed)
    depth = weights.shape[0]
    columns = groups * packed[0].shape[1]
    step = block_rows(positions, 320)
    steps = positions // step
    total = count * positions
    return pl.pallas_call(
        functools.partial(token_grad_body, blocks, groups, count, steps),
        grid=(count * steps,),
        in_specs=[
            pl.BlockSpec((step, columns // groups), lambda i: (i + first * steps, 0))
        ] * groups
        + [pl.BlockSpec(weights.shape, lambda i: (0, 0))],
        out_specs=piece_specs(count, steps, step, depth),
        out_shape=[jax.ShapeDtypeStruct((positions, depth), BF16)] * count,
        compiler_params=pltpu.CompilerParams(vmem_limit_bytes=VMEM_BYTES),
        cost_estimate=pl.CostEstimate(
            flops=2 * total * depth * columns,
            bytes_accessed=2 * (total * depth + depth * columns + total * columns),
            transcendentals=0,
        ),
        name="token_grad",
    )(*packed, weights)


def local(seq_size, fsdp_size, activations, cotangent, gain_attn, w_qkv, w_attn_out, gain_mlp, w_in, w_mlp_out):
    _, positions, width = activations.shape
    shard = w_qkv.shape[0]
    ff_shard = w_mlp_out.shape[0]
    local_width = width // seq_size
    length = positions * seq_size
    half = seq_size // 2
    lanes = min(128, local_width)
    groups = local_width // lanes
    me = lax.axis_index("seq")
    row = lax.axis_index("fsdp")
    after = lax.optimization_barrier


    def swap(values, axis, size, offset):
        return lax.ppermute(values, axis, [(i, i ^ offset) for i in range(size)])

    def swap_seq(values, offset):
        return swap(values, "seq", seq_size, offset)

    def spread(values):
        pieces = [values]
        bit = 1
        while bit < half:
            pieces = pieces + [swap_seq(piece, bit) for piece in pieces]
            bit *= 2
        return pieces

    def gather_seq(values):
        return spread(values) + spread(swap_seq(values, half))

    def fold(pieces):
        pieces = list(pieces)
        while len(pieces) > 1:
            left = len(pieces) // 2
            got = [swap_seq(piece.astype(BF16), left) for piece in pieces[left:]]
            pieces = [kept.astype(F32) + other.astype(F32) for kept, other in zip(pieces, got)]
        return pieces[0].astype(F32)

    def far_sum(pieces):
        return swap_seq(fold(pieces).astype(BF16), half)

    def exchange_seq(pieces):
        return [pieces[0]] + [swap_seq(pieces[k], k) for k in range(1, seq_size)]

    def by_member(pieces):
        stacked = jnp.stack(pieces)
        return [
            lax.dynamic_index_in_dim(stacked, me ^ member, 0, keepdims=False)
            for member in range(seq_size)
        ]

    def gather_fsdp(values):
        bit = fsdp_size // 2
        while bit:
            other = swap(values, "fsdp", fsdp_size, bit)
            high = (row & bit) != 0
            values = jnp.concatenate(
                [jnp.where(high, other, values), jnp.where(high, values, other)], 0
            )
            bit //= 2
        return values

    def halve_fsdp(values, bit):
        size = values.shape[0] // 2
        mine = jnp.where((row & bit) != 0, size, 0)
        kept = lax.dynamic_slice(values, (mine, 0), (size, values.shape[1]))
        sent = lax.dynamic_slice(values, (size - mine, 0), (size, values.shape[1]))
        total = kept.astype(F32) + swap(sent, "fsdp", fsdp_size, bit).astype(F32)
        return total.astype(BF16)

    def reduce_fsdp(values):
        return lax.psum_scatter(values, "fsdp", scatter_dimension=0, tiled=True)

    own_gain_attn = gain_attn.astype(F32)[:, None]
    own_gain_mlp = gain_mlp.astype(F32)[:, None]

    qkv_slice = jnp.concatenate(
        [
            lax.dynamic_slice(
                w_qkv, (0, part * width + me * local_width + group * lanes), (shard, lanes)
            )
            for group in range(groups)
            for part in range(3)
        ],
        1,
    )
    qkv_slice = (qkv_slice.astype(F32) * own_gain_attn).astype(BF16)
    attn_out_slice = lax.dynamic_slice(w_attn_out, (0, me * local_width), (shard, local_width))
    attn_weights = gather_fsdp(jnp.concatenate([qkv_slice, attn_out_slice], 1))
    packed_width = 3 * local_width

    tokens = activations.reshape(positions, width).astype(F32)
    xhat, inverse = centred_stats(tokens)
    own_x = xhat.astype(BF16)
    far_x = swap_seq(own_x, half)
    near_x_pieces = spread(own_x)
    far_x_pieces = spread(far_x)
    own_cotangent = cotangent.reshape(positions, width)
    near_c_pieces = spread(own_cotangent)

    unit_share = -(-ff_shard // seq_size)
    unit_share = -(-unit_share // ROW_TILE) * ROW_TILE
    padding = unit_share * seq_size - ff_shard
    units = fsdp_size * unit_share
    mlp_out_slice = lax.dynamic_slice(
        jnp.pad(w_mlp_out, ((0, padding), (0, 0))), (me * unit_share, 0), (unit_share, width)
    )
    in_slice = jnp.pad(
        w_in.reshape(shard, 2 * fsdp_size, ff_shard), ((0, 0), (0, 0), (0, padding))
    )
    in_slice = lax.dynamic_slice(
        in_slice, (0, 0, me * unit_share), (shard, 2 * fsdp_size, unit_share)
    ).reshape(shard, 2 * units)
    in_slice = (in_slice.astype(F32) * own_gain_mlp).astype(BF16)
    sections = jnp.concatenate(
        [
            attn_weights[block * shard : (block + 1) * shard, packed_width:]
            for block in bit_reversed(fsdp_size)
        ],
        0,
    )
    mlp_slice = jnp.concatenate([in_slice, fold_rows(mlp_out_slice, shard)], 1)
    mlp_weights = lax.all_gather(after((mlp_slice, attn_weights))[0], "fsdp", axis=0, tiled=True)
    far_sections = swap_seq(after((sections, far_x))[0], half)
    far_c_pieces = spread(swap_seq(after((own_cotangent, far_sections))[0], half))

    lane = lax.broadcasted_iota(jnp.int32, (length, lanes), 1)
    at = lax.broadcasted_iota(jnp.int32, (length, lanes), 0)
    place = ((at // positions) ^ me) * positions + at % positions
    frequency = jnp.exp((lane % HALF).astype(F32) * (-2.0 * math.log(rope_base) / HEAD))
    angles = place.astype(F32) * frequency
    cosine = jnp.cos(angles)
    sine = jnp.sin(angles) * jnp.where(lane % HEAD < HALF, -1.0, 1.0)

    begun = qkv_heads(near_x_pieces, attn_weights, cosine, sine, fsdp_size, [])
    queries, keys, values, x_all = qkv_heads(
        far_x_pieces, attn_weights, cosine, sine, fsdp_size, begun
    )

    def row_pieces(array):
        return [array[k * positions : (k + 1) * positions] for k in range(seq_size)]

    heads = [attend(after((queries, far_sections))[0], keys, values, 0)]
    group_pieces = [exchange_seq(row_pieces(heads[0][0]))]
    for group in range(1, groups):
        heads.append(attend(after((queries, far_c_pieces[0], heads[0]))[0], keys, values, group))
        group_pieces.append(exchange_seq(row_pieces(heads[group][0])))
    attn_out_full = jnp.concatenate(by_member(spread(sections) + spread(far_sections)), 1)
    attended_pieces = [jnp.concatenate(pieces, 1) for pieces in zip(*group_pieces)]
    attn_out_ordered = jnp.concatenate(
        [
            lax.dynamic_slice(
                attn_out_full, ((me ^ member) * local_width, 0), (local_width, width)
            )
            for member in range(seq_size)
        ],
        0,
    )
    attended = jnp.concatenate(attended_pieces, 1)
    mixed = tokens + dot_nn(attended, attn_out_ordered)
    xhat_mlp, inverse_mlp = centred_stats(mixed)
    own_x_mlp = xhat_mlp.astype(BF16)
    far_x_mlp = swap_seq(own_x_mlp, half)
    begun, near_back, near_out = mlp(
        spread(own_x_mlp), near_c_pieces, mlp_weights, units, fsdp_size, length, []
    )
    far_x_mlp, begun = after((far_x_mlp, begun))
    (hidden, gate_up_grad, x_mlp_all, cotangent_all), far_back, far_out = mlp(
        spread(far_x_mlp), far_c_pieces, mlp_weights, units, fsdp_size, length, begun
    )
    back_far = far_sum(far_back)
    back_near = fold(near_back)
    grad_mlp_out = dot_tn(hidden, cotangent_all).astype(BF16)
    grad_in = dot_tn(x_mlp_all, gate_up_grad).astype(BF16)
    back_far, grad_mlp_out, grad_in = after((back_far, grad_mlp_out, grad_in))

    mixed_grad = own_cotangent.astype(F32) + norm_backward(
        back_near + back_far.astype(F32), xhat_mlp, inverse_mlp
    )
    mixed_low = mixed_grad.astype(BF16)
    attended_grad = dot_nt(mixed_low, attn_out_ordered).astype(BF16)
    grads = []
    for group in range(groups):
        columns = [k * local_width + group * lanes for k in range(seq_size)]
        pieces = [attended_grad[:, start : start + lanes] for start in columns]
        grads.append(jnp.concatenate(exchange_seq(pieces), 0))
    attended_natural = jnp.concatenate(by_member(attended_pieces), 1)
    grad_attn_out = dot_tn(reorder(attended_natural, fsdp_size), mixed_low).astype(BF16)
    grads[0], grad_attn_out = after((grads[0], grad_attn_out))
    column_pieces = [
        lax.dynamic_slice(grad_attn_out, (0, (me ^ k) * local_width), (width, local_width))
        for k in range(seq_size)
    ]
    near_attn_out = fold(column_pieces[:half])
    far_attn_out = fold(column_pieces[half:]).astype(BF16)
    sum_near_out = fold(near_out)
    sum_far_out = fold(far_out).astype(BF16)
    grads[0], sum_far_out, far_attn_out = after((grads[0], sum_far_out, far_attn_out))
    sum_far_out = swap_seq(sum_far_out, half)
    far_attn_out = swap_seq(far_attn_out, half)

    def back_of(group):
        out, lse = heads[group]
        return attend_back(queries, keys, values, grads[group], out, lse, cosine, sine, group)

    packed = [back_of(0)]
    packed[0], sum_far_out, far_attn_out = after((packed[0], sum_far_out, far_attn_out))
    output = (mixed + (sum_near_out + sum_far_out.astype(F32))).astype(BF16)
    grad_attn_out = (near_attn_out + far_attn_out.astype(F32)).astype(BF16)
    first_grads = jnp.concatenate(
        [dot_tn(x_all, packed[0]).astype(BF16), grad_attn_out], 1
    )
    sum_in = reduce_fsdp(grad_in)
    sum_mlp_out = reduce_fsdp(after((grad_mlp_out, grad_in))[0])
    reduced = [halve_fsdp(first_grads, 1)]
    for group in range(1, groups):
        grads[group], output, first_grads, sum_in = after(
            (grads[group], output, first_grads, sum_in)
        )
        packed.append(back_of(group))

    far_grads = token_grad(packed, attn_weights, fsdp_size, half, positions, half)
    far_grads = fold(far_grads).astype(BF16)
    near_grads = token_grad(packed, attn_weights, fsdp_size, half, positions, 0)
    if groups > 1:
        last_grads = [dot_tn(x_all, section).astype(BF16) for section in packed[1:]]
        last_grads, far_grads = after((last_grads, far_grads))
        reduced += [halve_fsdp(section, 1) for section in last_grads]
    reduced[-1], sum_mlp_out = after((reduced[-1], sum_mlp_out))
    far_grads = swap_seq(far_grads, half)
    normed_grad = far_grads.astype(F32) + fold(near_grads)
    d_input = (mixed_grad + norm_backward(normed_grad, xhat, inverse)).astype(BF16)
    reduced = jnp.concatenate(reduced, 1)
    bit = 2
    while bit < fsdp_size:
        reduced = halve_fsdp(reduced, bit)
        bit *= 2

    in_pieces = by_member(gather_seq(sum_in))
    all_in = jnp.concatenate(
        [piece.reshape(shard, 2 * fsdp_size, unit_share) for piece in in_pieces], 2
    )
    all_in = all_in[:, :, :ff_shard].reshape(shard, -1).astype(F32)
    all_mlp_out = jnp.concatenate(by_member(gather_seq(sum_mlp_out)), 0)[:ff_shard].astype(F32)
    pieces = by_member(gather_seq(reduced))
    section = 3 * lanes
    all_attn_out = jnp.concatenate(
        [piece[:, section : section + local_width] for piece in pieces], 1
    ).astype(F32)
    starts = [0] + [section * group + local_width for group in range(1, groups)]
    all_qkv = jnp.concatenate(
        [
            piece[:, start + part * lanes : start + (part + 1) * lanes]
            for part in range(3)
            for piece in pieces
            for start in starts
        ],
        1,
    ).astype(F32)
    grad_gain_attn = jnp.sum(all_qkv * w_qkv.astype(F32), 1)
    grad_gain_mlp = jnp.sum(all_in * w_in.astype(F32), 1)
    return (
        output.reshape(activations.shape),
        d_input.reshape(activations.shape),
        grad_gain_attn,
        grad_gain_mlp,
        all_qkv * own_gain_attn,
        all_attn_out,
        all_in * own_gain_mlp,
        all_mlp_out,
    )


def solution(mesh):
    in_specs = (
        P("fsdp", "seq", None),
        P("fsdp", "seq", None),
        P("fsdp"),
        P("fsdp", None),
        P("fsdp", None),
        P("fsdp"),
        P("fsdp", None),
        P("fsdp", None),
    )
    out_specs = (
        P("fsdp", "seq", None),
        P("fsdp", "seq", None),
        P("fsdp"),
        P("fsdp"),
        P("fsdp", None),
        P("fsdp", None),
        P("fsdp", None),
        P("fsdp", None),
    )
    body = functools.partial(local, mesh.shape["seq"], mesh.shape["fsdp"])
    return jax.shard_map(body, mesh=mesh, in_specs=in_specs, out_specs=out_specs, check_vma=False)
```

```python
import functools
import math

import jax
import jax.numpy as jnp
from jax import lax
from jax.experimental import pallas as pl
from jax.experimental.pallas import tpu as pltpu
from jax.sharding import PartitionSpec as P

HEADS = 16
HEAD = 64
HALF = HEAD // 2
ROW_TILE = 16
BF16 = jnp.bfloat16
F32 = jnp.float32

eps = 1e-05
rope_base = 160000.0
VMEM_BYTES = 60 << 20


def dot_nn(a, b):
    return lax.dot_general(a, b, (((1,), (0,)), ((), ())), preferred_element_type=F32)


def dot_nt(a, b):
    return lax.dot_general(a, b, (((1,), (1,)), ((), ())), preferred_element_type=F32)


def dot_tn(a, b):
    return lax.dot_general(a, b, (((0,), (0,)), ((), ())), preferred_element_type=F32)


def block_rows(rows, wanted):
    best = rows
    for size in range(ROW_TILE, min(rows, wanted) + 1, ROW_TILE):
        if rows % size == 0:
            best = size
    return best


def centred_stats(values):
    average = jnp.mean(values, -1, keepdims=True)
    centred = values - average
    inverse = lax.rsqrt(jnp.mean(centred * centred, -1, keepdims=True) + eps)
    return centred * inverse, inverse


def norm_backward(grad, xhat, inverse):
    return inverse * (
        grad
        - jnp.mean(grad, -1, keepdims=True)
        - xhat * jnp.mean(grad * xhat, -1, keepdims=True)
    )


def partner(values):
    width = values.shape[-1]
    if width % 128:
        return jnp.concatenate([values[:, HALF:], values[:, :HALF]], 1)
    lane = lax.broadcasted_iota(jnp.int32, values.shape, 1)
    return jnp.where(
        lane % HEAD < HALF,
        pltpu.roll(values, width - HALF, 1),
        pltpu.roll(values, HALF, 1),
    )


def head_of_lane(shape):
    return lax.broadcasted_iota(jnp.int32, shape, 1) // HEAD


def only_head(values, head):
    return jnp.where(head_of_lane(values.shape) == head, values, jnp.zeros_like(values))


def take_piece(piece_refs, steps, scratch):
    for at, ref in enumerate(piece_refs):

        @pl.when(pl.program_id(0) // steps == at)
        def _(ref=ref):
            scratch[...] = ref[...]

    return scratch[...]


def piece_specs(count, steps, rows, columns):
    return [
        pl.BlockSpec(
            (rows, columns), lambda i, at=at: (jnp.clip(i - at * steps, 0, steps - 1), 0)
        )
        for at in range(count)
    ]


def bit_reversed(count):
    order = [0]
    while len(order) < count:
        order = [2 * at for at in order] + [2 * at + 1 for at in order]
    return order


def reorder(values, blocks):
    size = values.shape[1] // blocks
    return jnp.concatenate(
        [values[:, at * size : (at + 1) * size] for at in bit_reversed(blocks)], 1
    )


def qkv_body(blocks, count, steps, *refs):
    pieces, (w_ref, cos_ref, sin_ref) = refs[:count], refs[count : count + 3]
    q_ref, k_ref, v_ref, x_ref, scratch = refs[-5:]
    width = q_ref.shape[1]
    x = reorder(take_piece(pieces, steps, scratch), blocks)
    x_ref[...] = x
    packed = dot_nn(x, w_ref[...])
    cosine = cos_ref[...]
    sine = sin_ref[...]
    lanes = cosine.shape[1]
    for group in range(width // lanes):
        here = slice(group * lanes, (group + 1) * lanes)
        for at, ref in enumerate((q_ref, k_ref, v_ref)):
            start = (3 * group + at) * lanes
            part = packed[:, start : start + lanes]
            if at < 2:
                part = part * cosine + partner(part) * sine
            ref[:, here] = part.astype(BF16)


def qkv_heads(pieces, weights, cosine, sine, blocks, before):
    count = len(pieces)
    rows, depth = pieces[0].shape
    width = weights.shape[1] // 3
    step = block_rows(rows, 320)
    steps = rows // step
    length, table = cosine.shape
    first = count * steps if before else 0
    by_row = lambda columns: pl.BlockSpec((step, columns), lambda i: (i + first, 0))
    total = count * rows
    return pl.pallas_call(
        functools.partial(qkv_body, blocks, count, steps),
        grid=(count * steps,),
        in_specs=piece_specs(count, steps, step, depth)
        + [pl.BlockSpec(weights.shape, lambda i: (0, 0)), by_row(table), by_row(table)]
        + [pl.BlockSpec(memory_space=pl.ANY)] * len(before),
        out_specs=[by_row(width)] * 3 + [by_row(depth)],
        out_shape=[jax.ShapeDtypeStruct((length, width), BF16)] * 3
        + [jax.ShapeDtypeStruct((length, depth), BF16)],
        scratch_shapes=[pltpu.VMEM((step, depth), BF16)],
        input_output_aliases={count + 3 + at: at for at in range(len(before))},
        compiler_params=pltpu.CompilerParams(vmem_limit_bytes=VMEM_BYTES),
        cost_estimate=pl.CostEstimate(
            flops=6 * total * depth * width,
            bytes_accessed=2 * (2 * total * depth + 3 * depth * width + 3 * total * width),
            transcendentals=0,
        ),
        name="qkv_rope",
    )(*pieces, weights, cosine, sine, *before)


def attend_body(q_ref, k_ref, v_ref, out_ref, lse_ref):
    width = q_ref.shape[1]
    heads = width // HEAD
    queries = q_ref[...] * jnp.asarray(HEAD**-0.5, BF16)
    keys = k_ref[...]
    values = v_ref[...]
    outs, totals, peaks = [], [], []
    for head in range(heads):
        scores = dot_nt(keys, only_head(queries, head))
        peak = jnp.max(scores, 0, keepdims=True)
        exponent = jnp.exp(scores - peak)
        low = exponent.astype(BF16)
        if heads == 2:
            own = head_of_lane(values.shape) == head
            both = dot_tn(jnp.where(own, values, jnp.ones_like(values)), low)
            outs.append(both[head * HEAD : (head + 1) * HEAD])
            totals.append(both[(1 - head) * HEAD : (2 - head) * HEAD])
        else:
            outs.append(dot_tn(values, low)[head * HEAD : (head + 1) * HEAD])
            totals.append(
                jnp.broadcast_to(jnp.sum(exponent, 0, keepdims=True), outs[-1].shape)
            )
        peaks.append(jnp.broadcast_to(peak, outs[-1].shape))
    total = jnp.concatenate(totals, 0)
    out_ref[...] = (jnp.concatenate(outs, 0) / total).T.astype(BF16)
    lse_ref[...] = jnp.concatenate(peaks, 0) + jnp.log(total)


def attend(queries, keys, values, group):
    rows, local_width = queries.shape
    width = min(128, local_width)
    step = rows // 2
    q_spec = pl.BlockSpec((step, width), lambda i: (i, group))
    k_spec = pl.BlockSpec((rows, width), lambda i: (0, group))
    return pl.pallas_call(
        attend_body,
        grid=(rows // step,),
        in_specs=[q_spec, k_spec, k_spec],
        out_specs=[
            pl.BlockSpec((step, width), lambda i: (i, 0)),
            pl.BlockSpec((width, step), lambda i: (0, i)),
        ],
        out_shape=[
            jax.ShapeDtypeStruct((rows, width), BF16),
            jax.ShapeDtypeStruct((width, rows), F32),
        ],
        compiler_params=pltpu.CompilerParams(vmem_limit_bytes=VMEM_BYTES),
        cost_estimate=pl.CostEstimate(
            flops=16 * rows * rows * width,
            bytes_accessed=8 * rows * width,
            transcendentals=rows * rows * width // HEAD,
        ),
        name="attend",
    )(queries, keys, values)


def attend_back_body(
    q_ref, k_ref, v_ref, g_ref, out_ref, lse_ref, cos_ref, sin_ref, packed_ref, dk_sum, dv_sum
):
    step_rows, width = q_ref.shape
    step = pl.program_id(0)

    @pl.when(step == 0)
    def _():
        dk_sum[...] = jnp.zeros_like(dk_sum)
        dv_sum[...] = jnp.zeros_like(dv_sum)

    factor = HEAD**-0.5
    queries = q_ref[...] * jnp.asarray(factor, BF16)
    keys = k_ref[...]
    values = v_ref[...]
    grads = g_ref[...]
    product = (grads.astype(F32) * out_ref[...].astype(F32)).T
    dq = jnp.zeros(product.shape, F32)
    for head in range(width // HEAD):
        own_queries = only_head(queries, head)
        own_grads = only_head(grads, head)
        lse = lse_ref[head * HEAD : head * HEAD + 1, :]
        inner = jnp.sum(product[head * HEAD : (head + 1) * HEAD], 0, keepdims=True)
        probs = jnp.exp(dot_nt(keys, own_queries) - lse)
        prob_grad = dot_nt(values, own_grads)
        score_grad = (probs * (prob_grad - inner)).astype(BF16)
        dv_sum[...] += dot_nn(probs.astype(BF16), own_grads)
        dk_sum[...] += dot_nn(score_grad, own_queries)
        dq = dq + dot_tn(only_head(keys, head), score_grad)
    dq = (dq.T * factor).astype(BF16).astype(F32)
    here = pl.ds(pl.multiple_of(step * step_rows, ROW_TILE), step_rows)
    packed_ref[here, :width] = (dq * cos_ref[here, :] - partner(dq) * sin_ref[here, :]).astype(BF16)

    @pl.when(step == pl.num_programs(0) - 1)
    def _():
        dk = dk_sum[...].astype(BF16).astype(F32)
        packed_ref[:, width : 2 * width] = (
            dk * cos_ref[...] - partner(dk) * sin_ref[...]
        ).astype(BF16)
        packed_ref[:, 2 * width :] = dv_sum[...].astype(BF16)


def attend_back(queries, keys, values, grads, out, lse, cosine, sine, group):
    rows, local_width = queries.shape
    width = min(128, local_width)
    step = block_rows(rows, 512)
    q_spec = pl.BlockSpec((step, width), lambda i: (i, group))
    k_spec = pl.BlockSpec((rows, width), lambda i: (0, group))
    own_spec = pl.BlockSpec((step, width), lambda i: (i, 0))
    all_spec = pl.BlockSpec((rows, width), lambda i: (0, 0))
    return pl.pallas_call(
        attend_back_body,
        grid=(rows // step,),
        in_specs=[
            q_spec, k_spec, k_spec, own_spec, own_spec,
            pl.BlockSpec((width, step), lambda i: (0, i)),
            all_spec, all_spec,
        ],
        out_specs=pl.BlockSpec((rows, 3 * width), lambda i: (0, 0)),
        out_shape=jax.ShapeDtypeStruct((rows, 3 * width), BF16),
        scratch_shapes=[pltpu.VMEM((rows, width), F32)] * 2,
        compiler_params=pltpu.CompilerParams(vmem_limit_bytes=VMEM_BYTES),
        cost_estimate=pl.CostEstimate(
            flops=40 * rows * rows * width,
            bytes_accessed=20 * rows * width,
            transcendentals=rows * rows * width // HEAD,
        ),
        name="attend_back",
    )(queries, keys, values, grads, out, lse, cosine, sine)


def mlp_body(count, steps, blocks, units, *refs):
    x_pieces, c_pieces = refs[:count], refs[count : 2 * count]
    weights_ref = refs[2 * count]
    x_scratch, c_scratch, wo_ref = refs[-3:]
    results = refs[-3 - 4 - 2 * count : -3]
    wi_ref = weights_ref.at[:, : 2 * units]
    depth = wo_ref.shape[1]

    @pl.when(pl.program_id(0) == 0)
    def _():
        shard, share = depth // blocks, units // blocks
        rows = math.gcd(share, shard)
        wide = depth * rows // shard
        for block in range(blocks):
            for tall in range(share // rows):
                for at in range(shard // rows):
                    wo_ref[
                        pl.ds(block * share + tall * rows, rows), at * wide : (at + 1) * wide
                    ] = weights_ref[
                        pl.ds(block * shard + at * rows, rows),
                        2 * units + tall * wide : 2 * units + (tall + 1) * wide,
                    ]

    hidden_ref, gate_up_ref, x_ref, c_ref = results[:4]
    back_refs, out_refs = results[4 : 4 + count], results[4 + count :]
    x = take_piece(x_pieces, steps, x_scratch)
    cotangent = take_piece(c_pieces, steps, c_scratch)
    x_ref[...] = x
    c_ref[...] = cotangent
    gate_up = dot_nn(x, wi_ref[...])
    hidden_grad = dot_nt(cotangent, wo_ref[...])
    gate = gate_up[:, :units]
    up = gate_up[:, units:]
    share = 0.5 * (1.0 + lax.erf(gate * 2.0**-0.5))
    activated = gate * share
    slope = share + gate * jnp.exp(-0.5 * gate * gate) * (2.0 * math.pi) ** -0.5
    hidden = (activated * up).astype(BF16)
    hidden_ref[...] = hidden
    gate_grad = (hidden_grad * up * slope).astype(BF16)
    up_grad = (hidden_grad * activated).astype(BF16)
    both = jnp.concatenate([gate_grad, up_grad], 1)
    gate_up_ref[...] = both
    back = dot_nt(both, wi_ref[...]).astype(BF16)
    out = dot_nn(hidden, wo_ref[...]).astype(BF16)
    for at in range(count):

        @pl.when(pl.program_id(0) // steps == at)
        def _(at=at):
            back_refs[at][...] = back
            out_refs[at][...] = out


def fold_rows(values, shard):
    share, depth = values.shape
    rows = math.gcd(share, shard)
    tall, wide = share // rows, shard // rows
    return (
        values.reshape(tall, rows, wide, depth // wide)
        .transpose(2, 1, 0, 3)
        .reshape(shard, tall * depth // wide)
    )


def mlp(x_pieces, c_pieces, weights, units, blocks, length, before):
    count = len(x_pieces)
    rows, depth = x_pieces[0].shape
    step = block_rows(rows, 320)
    steps = rows // step
    total = count * rows
    first = count * steps if before else 0
    by_row = lambda columns: pl.BlockSpec((step, columns), lambda i: (i + first, 0))
    whole = lambda shape: pl.BlockSpec(shape, lambda i: (0, 0))
    pieces = piece_specs(count, steps, step, depth)
    results = pl.pallas_call(
        functools.partial(mlp_body, count, steps, blocks, units),
        grid=(count * steps,),
        in_specs=pieces
        + pieces
        + [whole(weights.shape)]
        + [pl.BlockSpec(memory_space=pl.ANY)] * len(before),
        out_specs=[by_row(units), by_row(2 * units), by_row(depth), by_row(depth)]
        + pieces
        + pieces,
        out_shape=[
            jax.ShapeDtypeStruct((length, columns), BF16)
            for columns in (units, 2 * units, depth, depth)
        ]
        + [jax.ShapeDtypeStruct((rows, depth), BF16)] * (2 * count),
        scratch_shapes=[pltpu.VMEM((step, depth), BF16)] * 2 + [pltpu.VMEM((units, depth), BF16)],
        input_output_aliases={2 * count + 1 + at: at for at in range(len(before))},
        compiler_params=pltpu.CompilerParams(vmem_limit_bytes=VMEM_BYTES),
        cost_estimate=pl.CostEstimate(
            flops=12 * total * depth * units,
            bytes_accessed=2 * total * (6 * depth + 3 * units) + 6 * depth * units,
            transcendentals=2 * total * units,
        ),
        name="mlp",
    )(*x_pieces, *c_pieces, weights, *before)
    return results[:4], results[4 : 4 + count], results[4 + count :]


def token_grad_body(blocks, groups, count, steps, *refs):
    packed = jnp.concatenate([ref[...] for ref in refs[:groups]], 1)
    results = refs[groups + 1 :]
    grad = reorder(dot_nt(packed, refs[groups][...]).astype(BF16), blocks)
    for at in range(count):

        @pl.when(pl.program_id(0) // steps == at)
        def _(at=at):
            results[at][...] = grad


def token_grad(packed, weights, blocks, count, positions, first):
    groups = len(packed)
    depth = weights.shape[0]
    columns = groups * packed[0].shape[1]
    step = block_rows(positions, 320)
    steps = positions // step
    total = count * positions
    return pl.pallas_call(
        functools.partial(token_grad_body, blocks, groups, count, steps),
        grid=(count * steps,),
        in_specs=[
            pl.BlockSpec((step, columns // groups), lambda i: (i + first * steps, 0))
        ] * groups
        + [pl.BlockSpec(weights.shape, lambda i: (0, 0))],
        out_specs=piece_specs(count, steps, step, depth),
        out_shape=[jax.ShapeDtypeStruct((positions, depth), BF16)] * count,
        compiler_params=pltpu.CompilerParams(vmem_limit_bytes=VMEM_BYTES),
        cost_estimate=pl.CostEstimate(
            flops=2 * total * depth * columns,
            bytes_accessed=2 * (total * depth + depth * columns + total * columns),
            transcendentals=0,
        ),
        name="token_grad",
    )(*packed, weights)


def local(seq_size, fsdp_size, activations, cotangent, gain_attn, w_qkv, w_attn_out, gain_mlp, w_in, w_mlp_out):
    _, positions, width = activations.shape
    shard = w_qkv.shape[0]
    ff_shard = w_mlp_out.shape[0]
    local_width = width // seq_size
    length = positions * seq_size
    half = seq_size // 2
    lanes = min(128, local_width)
    groups = local_width // lanes
    me = lax.axis_index("seq")
    row = lax.axis_index("fsdp")
    after = lax.optimization_barrier


    def swap(values, axis, size, offset):
        return lax.ppermute(values, axis, [(i, i ^ offset) for i in range(size)])

    def swap_seq(values, offset):
        return swap(values, "seq", seq_size, offset)

    def spread(values):
        pieces = [values]
        bit = 1
        while bit < half:
            pieces = pieces + [swap_seq(piece, bit) for piece in pieces]
            bit *= 2
        return pieces

    def gather_seq(values):
        return spread(values) + spread(swap_seq(values, half))

    def fold(pieces):
        pieces = list(pieces)
        while len(pieces) > 1:
            left = len(pieces) // 2
            got = [swap_seq(piece.astype(BF16), left) for piece in pieces[left:]]
            pieces = [kept.astype(F32) + other.astype(F32) for kept, other in zip(pieces, got)]
        return pieces[0].astype(F32)

    def far_sum(pieces):
        return swap_seq(fold(pieces).astype(BF16), half)

    def exchange_seq(pieces):
        return [pieces[0]] + [swap_seq(pieces[k], k) for k in range(1, seq_size)]

    def by_member(pieces):
        stacked = jnp.stack(pieces)
        return [
            lax.dynamic_index_in_dim(stacked, me ^ member, 0, keepdims=False)
            for member in range(seq_size)
        ]

    def double_fsdp(values, bit):
        other = swap(values, "fsdp", fsdp_size, bit)
        high = (row & bit) != 0
        return jnp.concatenate(
            [jnp.where(high, other, values), jnp.where(high, values, other)], 0
        )

    def halve_fsdp(values, bit, joined=lambda got: got):
        size = values.shape[0] // 2
        mine = jnp.where((row & bit) != 0, size, 0)
        kept = lax.dynamic_slice(values, (mine, 0), (size, values.shape[1]))
        sent = lax.dynamic_slice(values, (size - mine, 0), (size, values.shape[1]))
        got = joined(swap(sent, "fsdp", fsdp_size, bit))
        return (kept.astype(F32) + got.astype(F32)).astype(BF16)

    def reduce_fsdp(values):
        return lax.psum_scatter(values, "fsdp", scatter_dimension=0, tiled=True)

    own_gain_attn = gain_attn.astype(F32)[:, None]
    own_gain_mlp = gain_mlp.astype(F32)[:, None]

    qkv_slice = jnp.concatenate(
        [
            lax.dynamic_slice(
                w_qkv, (0, part * width + me * local_width + group * lanes), (shard, lanes)
            )
            for group in range(groups)
            for part in range(3)
        ],
        1,
    )
    qkv_slice = (qkv_slice.astype(F32) * own_gain_attn).astype(BF16)
    attn_out_slice = lax.dynamic_slice(w_attn_out, (0, me * local_width), (shard, local_width))

    tokens = activations.reshape(positions, width).astype(F32)
    xhat, inverse = centred_stats(tokens)
    own_x = xhat.astype(BF16)
    far_x = swap_seq(own_x, half)
    near_x_pieces = spread(own_x)
    far_x_pieces = spread(far_x)
    own_cotangent = cotangent.reshape(positions, width)
    near_c_pieces = spread(own_cotangent)

    unit_share = -(-ff_shard // seq_size)
    unit_share = -(-unit_share // ROW_TILE) * ROW_TILE
    padding = unit_share * seq_size - ff_shard
    units = fsdp_size * unit_share
    mlp_out_slice = lax.dynamic_slice(
        jnp.pad(w_mlp_out, ((0, padding), (0, 0))), (me * unit_share, 0), (unit_share, width)
    )
    in_slice = jnp.pad(
        w_in.reshape(shard, 2 * fsdp_size, ff_shard), ((0, 0), (0, 0), (0, padding))
    )
    in_slice = lax.dynamic_slice(
        in_slice, (0, 0, me * unit_share), (shard, 2 * fsdp_size, unit_share)
    ).reshape(shard, 2 * units)
    in_slice = (in_slice.astype(F32) * own_gain_mlp).astype(BF16)
    lane = lax.broadcasted_iota(jnp.int32, (length, lanes), 1)
    at = lax.broadcasted_iota(jnp.int32, (length, lanes), 0)
    place = ((at // positions) ^ me) * positions + at % positions
    frequency = jnp.exp((lane % HALF).astype(F32) * (-2.0 * math.log(rope_base) / HEAD))
    angles = place.astype(F32) * frequency
    cosine = jnp.cos(angles)
    sine = jnp.sin(angles) * jnp.where(lane % HEAD < HALF, -1.0, 1.0)

    bit = fsdp_size // 2
    qkv_weights, sections = qkv_slice, attn_out_slice
    while bit:
        if bit == 1:
            qkv_weights, cosine, sine = after((qkv_weights, cosine, sine))
        doubled = double_fsdp(qkv_weights, bit)
        if bit < fsdp_size // 2:
            sections, qkv_weights = after((sections, qkv_weights))
            sections = double_fsdp(sections, 2 * bit)
        qkv_weights = doubled
        bit //= 2
    sections = double_fsdp(after((sections, qkv_weights))[0], 1)
    sections = jnp.concatenate(
        [sections[block * shard : (block + 1) * shard] for block in bit_reversed(fsdp_size)], 0
    )
    mlp_slice = jnp.concatenate([in_slice, fold_rows(mlp_out_slice, shard)], 1)
    mlp_weights = lax.all_gather(after((mlp_slice, qkv_weights))[0], "fsdp", axis=0, tiled=True)
    far_sections = swap_seq(after((sections, far_x))[0], half)
    far_c_pieces = spread(swap_seq(after((own_cotangent, far_sections))[0], half))

    begun = qkv_heads(near_x_pieces, qkv_weights, cosine, sine, fsdp_size, [])
    queries, keys, values, x_all = qkv_heads(
        far_x_pieces, qkv_weights, cosine, sine, fsdp_size, begun
    )

    def row_pieces(array):
        return [array[k * positions : (k + 1) * positions] for k in range(seq_size)]

    heads = [attend(after((queries, far_sections))[0], keys, values, 0)]
    group_pieces = [exchange_seq(row_pieces(heads[0][0]))]
    for group in range(1, groups):
        heads.append(attend(after((queries, far_c_pieces[0], heads[0]))[0], keys, values, group))
        group_pieces.append(exchange_seq(row_pieces(heads[group][0])))
    attn_out_full = jnp.concatenate(by_member(spread(sections) + spread(far_sections)), 1)
    attended_pieces = [jnp.concatenate(pieces, 1) for pieces in zip(*group_pieces)]
    attn_out_ordered = jnp.concatenate(
        [
            lax.dynamic_slice(
                attn_out_full, ((me ^ member) * local_width, 0), (local_width, width)
            )
            for member in range(seq_size)
        ],
        0,
    )
    attended = jnp.concatenate(attended_pieces, 1)
    mixed = tokens + dot_nn(attended, attn_out_ordered)
    xhat_mlp, inverse_mlp = centred_stats(mixed)
    own_x_mlp = xhat_mlp.astype(BF16)
    far_x_mlp = swap_seq(own_x_mlp, half)
    begun, near_back, near_out = mlp(
        spread(own_x_mlp), near_c_pieces, mlp_weights, units, fsdp_size, length, []
    )
    far_x_mlp, begun = after((far_x_mlp, begun))
    (hidden, gate_up_grad, x_mlp_all, cotangent_all), far_back, far_out = mlp(
        spread(far_x_mlp), far_c_pieces, mlp_weights, units, fsdp_size, length, begun
    )
    back_far = far_sum(far_back)
    back_near = fold(near_back)
    grad_mlp_out = dot_tn(hidden, cotangent_all).astype(BF16)
    grad_in = dot_tn(x_mlp_all, gate_up_grad).astype(BF16)
    back_far, grad_mlp_out, grad_in = after((back_far, grad_mlp_out, grad_in))

    mixed_grad = own_cotangent.astype(F32) + norm_backward(
        back_near + back_far.astype(F32), xhat_mlp, inverse_mlp
    )
    mixed_low = mixed_grad.astype(BF16)
    attended_grad = dot_nt(mixed_low, attn_out_ordered).astype(BF16)
    grads = []
    for group in range(groups):
        columns = [k * local_width + group * lanes for k in range(seq_size)]
        pieces = [attended_grad[:, start : start + lanes] for start in columns]
        grads.append(jnp.concatenate(exchange_seq(pieces), 0))
    attended_natural = jnp.concatenate(by_member(attended_pieces), 1)
    grad_attn_out = dot_tn(reorder(attended_natural, fsdp_size), mixed_low).astype(BF16)
    grads[0], grad_attn_out = after((grads[0], grad_attn_out))
    column_pieces = [
        lax.dynamic_slice(grad_attn_out, (0, (me ^ k) * local_width), (width, local_width))
        for k in range(seq_size)
    ]
    near_attn_out = fold(column_pieces[:half])
    far_attn_out = fold(column_pieces[half:]).astype(BF16)
    sum_near_out = fold(near_out)
    sum_far_out = fold(far_out).astype(BF16)
    grads[0], sum_far_out, far_attn_out = after((grads[0], sum_far_out, far_attn_out))
    sum_far_out = swap_seq(sum_far_out, half)
    far_attn_out = swap_seq(far_attn_out, half)

    def back_of(group):
        out, lse = heads[group]
        return attend_back(queries, keys, values, grads[group], out, lse, cosine, sine, group)

    packed = [back_of(0)]
    packed[0], sum_far_out, far_attn_out = after((packed[0], sum_far_out, far_attn_out))
    output = (mixed + (sum_near_out + sum_far_out.astype(F32))).astype(BF16)
    grad_attn_out = (near_attn_out + far_attn_out.astype(F32)).astype(BF16)
    first_grads = jnp.concatenate(
        [dot_tn(x_all, packed[0]).astype(BF16), grad_attn_out], 1
    )
    sum_in = reduce_fsdp(grad_in)
    sum_mlp_out = reduce_fsdp(after((grad_mlp_out, grad_in))[0])
    for group in range(1, groups):
        grads[group], output, _, sum_in = after(
            (grads[group], output, first_grads, sum_in)
        )
        packed.append(back_of(group))
    reduced = [halve_fsdp(first_grads, 1, lambda got: after((got, packed[-1]))[0])]

    later_bits = [1 << at for at in range(1, fsdp_size.bit_length() - 1)]
    chains = [later_bits] + [[1] + later_bits] * (groups - 1)
    last_grads = [dot_tn(x_all, section).astype(BF16) for section in packed[1:]]
    packed, last_grads, reduced = after((packed, last_grads, reduced))
    reduced = reduced + last_grads
    cuts = [0, positions // 4, positions // 2, positions]
    near_grads, far_parts = None, None
    for stage in range(max(len(chain) for chain in chains)):
        if stage == 0:
            far_grads = fold(
                token_grad(packed, qkv_weights, fsdp_size, half, positions, half)
            ).astype(BF16)
        if stage == 1:
            far_parts = [
                swap_seq(far_grads[start:end], half) for start, end in zip(cuts, cuts[1:])
            ]
            near_grads = token_grad(packed, qkv_weights, fsdp_size, half, positions, 0)
        if stage == 2:
            near_grads = fold(near_grads)
        reduced = [
            halve_fsdp(section, chain[stage]) if stage < len(chain) else section
            for section, chain in zip(reduced, chains)
        ]
        if stage == 0:
            reduced, far_grads, packed = after((reduced, far_grads, packed))
        if stage == 1:
            reduced, near_grads, sum_mlp_out, far_parts[0] = after(
                (reduced, near_grads, sum_mlp_out, far_parts[0])
            )
        if stage == 2:
            reduced, near_grads, far_parts[1] = after((reduced, near_grads, far_parts[1]))
    if not isinstance(near_grads, jax.Array):
        near_grads = fold(near_grads)
    reduced = jnp.concatenate(reduced, 1)
    far_reduced = swap_seq(reduced, half)
    far_reduced, far_parts = after((far_reduced, far_parts))
    sum_mlp_out = after((sum_mlp_out, far_parts[0]))[0]
    normed_grad = jnp.concatenate(far_parts, 0).astype(F32) + near_grads
    d_input = (mixed_grad + norm_backward(normed_grad, xhat, inverse)).astype(BF16)

    in_pieces = by_member(gather_seq(sum_in))
    all_in = jnp.concatenate(
        [piece.reshape(shard, 2 * fsdp_size, unit_share) for piece in in_pieces], 2
    )
    all_in = all_in[:, :, :ff_shard].reshape(shard, -1).astype(F32)
    all_mlp_out = jnp.concatenate(by_member(gather_seq(sum_mlp_out)), 0)[:ff_shard].astype(F32)
    pieces = by_member(spread(reduced) + spread(far_reduced))
    section = 3 * lanes
    all_attn_out = jnp.concatenate(
        [piece[:, section : section + local_width] for piece in pieces], 1
    ).astype(F32)
    starts = [0] + [section * group + local_width for group in range(1, groups)]
    all_qkv = jnp.concatenate(
        [
            piece[:, start + part * lanes : start + (part + 1) * lanes]
            for part in range(3)
            for piece in pieces
            for start in starts
        ],
        1,
    ).astype(F32)
    grad_gain_attn = jnp.sum(all_qkv * w_qkv.astype(F32), 1)
    grad_gain_mlp = jnp.sum(all_in * w_in.astype(F32), 1)
    return (
        output.reshape(activations.shape),
        d_input.reshape(activations.shape),
        grad_gain_attn,
        grad_gain_mlp,
        all_qkv * own_gain_attn,
        all_attn_out,
        all_in * own_gain_mlp,
        all_mlp_out,
    )


def solution(mesh):
    in_specs = (
        P("fsdp", "seq", None),
        P("fsdp", "seq", None),
        P("fsdp"),
        P("fsdp", None),
        P("fsdp", None),
        P("fsdp"),
        P("fsdp", None),
        P("fsdp", None),
    )
    out_specs = (
        P("fsdp", "seq", None),
        P("fsdp", "seq", None),
        P("fsdp"),
        P("fsdp"),
        P("fsdp", None),
        P("fsdp", None),
        P("fsdp", None),
        P("fsdp", None),
    )
    body = functools.partial(local, mesh.shape["seq"], mesh.shape["fsdp"])
    return jax.shard_map(body, mesh=mesh, in_specs=in_specs, out_specs=out_specs, check_vma=False)
```

```python
import functools
import math

import jax
import jax.numpy as jnp
from jax import lax
from jax.experimental import pallas as pl
from jax.experimental.pallas import tpu as pltpu
from jax.sharding import PartitionSpec as P

HEADS = 16
HEAD = 64
HALF = HEAD // 2
ROW_TILE = 16
BF16 = jnp.bfloat16
F32 = jnp.float32

eps = 1e-05
rope_base = 160000.0
VMEM_BYTES = 60 << 20


def dot_nn(a, b):
    return lax.dot_general(a, b, (((1,), (0,)), ((), ())), preferred_element_type=F32)


def dot_nt(a, b):
    return lax.dot_general(a, b, (((1,), (1,)), ((), ())), preferred_element_type=F32)


def dot_tn(a, b):
    return lax.dot_general(a, b, (((0,), (0,)), ((), ())), preferred_element_type=F32)


def block_rows(rows, wanted):
    best = rows
    for size in range(ROW_TILE, min(rows, wanted) + 1, ROW_TILE):
        if rows % size == 0:
            best = size
    return best


def centred_stats(values):
    average = jnp.mean(values, -1, keepdims=True)
    centred = values - average
    inverse = lax.rsqrt(jnp.mean(centred * centred, -1, keepdims=True) + eps)
    return centred * inverse, inverse


def norm_backward(grad, xhat, inverse):
    return inverse * (
        grad
        - jnp.mean(grad, -1, keepdims=True)
        - xhat * jnp.mean(grad * xhat, -1, keepdims=True)
    )


def partner(values):
    width = values.shape[-1]
    if width % 128:
        return jnp.concatenate([values[:, HALF:], values[:, :HALF]], 1)
    lane = lax.broadcasted_iota(jnp.int32, values.shape, 1)
    return jnp.where(
        lane % HEAD < HALF,
        pltpu.roll(values, width - HALF, 1),
        pltpu.roll(values, HALF, 1),
    )


def head_of_lane(shape):
    return lax.broadcasted_iota(jnp.int32, shape, 1) // HEAD


def only_head(values, head):
    return jnp.where(head_of_lane(values.shape) == head, values, jnp.zeros_like(values))


def take_piece(piece_refs, steps, scratch):
    for at, ref in enumerate(piece_refs):

        @pl.when(pl.program_id(0) // steps == at)
        def _(ref=ref):
            scratch[...] = ref[...]

    return scratch[...]


def piece_specs(count, steps, rows, columns):
    return [
        pl.BlockSpec(
            (rows, columns), lambda i, at=at: (jnp.clip(i - at * steps, 0, steps - 1), 0)
        )
        for at in range(count)
    ]


def bit_reversed(count):
    order = [0]
    while len(order) < count:
        order = [2 * at for at in order] + [2 * at + 1 for at in order]
    return order


def reorder(values, blocks):
    size = values.shape[1] // blocks
    return jnp.concatenate(
        [values[:, at * size : (at + 1) * size] for at in bit_reversed(blocks)], 1
    )


def qkv_body(blocks, count, steps, *refs):
    pieces, (w_ref, cos_ref, sin_ref) = refs[:count], refs[count : count + 3]
    q_ref, k_ref, v_ref, x_ref, scratch = refs[-5:]
    width = q_ref.shape[1]
    x = reorder(take_piece(pieces, steps, scratch), blocks)
    x_ref[...] = x
    packed = dot_nn(x, w_ref[...])
    cosine = cos_ref[...]
    sine = sin_ref[...]
    lanes = cosine.shape[1]
    for group in range(width // lanes):
        here = slice(group * lanes, (group + 1) * lanes)
        for at, ref in enumerate((q_ref, k_ref, v_ref)):
            start = (3 * group + at) * lanes
            part = packed[:, start : start + lanes]
            if at < 2:
                part = part * cosine + partner(part) * sine
            ref[:, here] = part.astype(BF16)


def qkv_heads(pieces, weights, cosine, sine, blocks, before):
    count = len(pieces)
    rows, depth = pieces[0].shape
    width = weights.shape[1] // 3
    step = block_rows(rows, 320)
    steps = rows // step
    length, table = cosine.shape
    first = count * steps if before else 0
    by_row = lambda columns: pl.BlockSpec((step, columns), lambda i: (i + first, 0))
    total = count * rows
    return pl.pallas_call(
        functools.partial(qkv_body, blocks, count, steps),
        grid=(count * steps,),
        in_specs=piece_specs(count, steps, step, depth)
        + [pl.BlockSpec(weights.shape, lambda i: (0, 0)), by_row(table), by_row(table)]
        + [pl.BlockSpec(memory_space=pl.ANY)] * len(before),
        out_specs=[by_row(width)] * 3 + [by_row(depth)],
        out_shape=[jax.ShapeDtypeStruct((length, width), BF16)] * 3
        + [jax.ShapeDtypeStruct((length, depth), BF16)],
        scratch_shapes=[pltpu.VMEM((step, depth), BF16)],
        input_output_aliases={count + 3 + at: at for at in range(len(before))},
        compiler_params=pltpu.CompilerParams(vmem_limit_bytes=VMEM_BYTES),
        cost_estimate=pl.CostEstimate(
            flops=6 * total * depth * width,
            bytes_accessed=2 * (2 * total * depth + 3 * depth * width + 3 * total * width),
            transcendentals=0,
        ),
        name="qkv_rope",
    )(*pieces, weights, cosine, sine, *before)


def attend_body(q_ref, k_ref, v_ref, out_ref, lse_ref):
    width = q_ref.shape[1]
    heads = width // HEAD
    queries = q_ref[...] * jnp.asarray(HEAD**-0.5, BF16)
    keys = k_ref[...]
    values = v_ref[...]
    outs, totals, peaks = [], [], []
    for head in range(heads):
        scores = dot_nt(keys, only_head(queries, head))
        peak = jnp.max(scores, 0, keepdims=True)
        exponent = jnp.exp(scores - peak)
        low = exponent.astype(BF16)
        if heads == 2:
            own = head_of_lane(values.shape) == head
            both = dot_tn(jnp.where(own, values, jnp.ones_like(values)), low)
            outs.append(both[head * HEAD : (head + 1) * HEAD])
            totals.append(both[(1 - head) * HEAD : (2 - head) * HEAD])
        else:
            outs.append(dot_tn(values, low)[head * HEAD : (head + 1) * HEAD])
            totals.append(
                jnp.broadcast_to(jnp.sum(exponent, 0, keepdims=True), outs[-1].shape)
            )
        peaks.append(jnp.broadcast_to(peak, outs[-1].shape))
    total = jnp.concatenate(totals, 0)
    out_ref[...] = (jnp.concatenate(outs, 0) / total).T.astype(BF16)
    lse_ref[...] = jnp.concatenate(peaks, 0) + jnp.log(total)


def attend(queries, keys, values, group):
    rows, local_width = queries.shape
    width = min(128, local_width)
    step = rows // 2
    q_spec = pl.BlockSpec((step, width), lambda i: (i, group))
    k_spec = pl.BlockSpec((rows, width), lambda i: (0, group))
    return pl.pallas_call(
        attend_body,
        grid=(rows // step,),
        in_specs=[q_spec, k_spec, k_spec],
        out_specs=[
            pl.BlockSpec((step, width), lambda i: (i, 0)),
            pl.BlockSpec((width, step), lambda i: (0, i)),
        ],
        out_shape=[
            jax.ShapeDtypeStruct((rows, width), BF16),
            jax.ShapeDtypeStruct((width, rows), F32),
        ],
        compiler_params=pltpu.CompilerParams(vmem_limit_bytes=VMEM_BYTES),
        cost_estimate=pl.CostEstimate(
            flops=16 * rows * rows * width,
            bytes_accessed=8 * rows * width,
            transcendentals=rows * rows * width // HEAD,
        ),
        name="attend",
    )(queries, keys, values)


def attend_back_body(
    q_ref, k_ref, v_ref, g_ref, out_ref, lse_ref, cos_ref, sin_ref, packed_ref, dk_sum, dv_sum
):
    step_rows, width = q_ref.shape
    step = pl.program_id(0)

    @pl.when(step == 0)
    def _():
        dk_sum[...] = jnp.zeros_like(dk_sum)
        dv_sum[...] = jnp.zeros_like(dv_sum)

    factor = HEAD**-0.5
    queries = q_ref[...] * jnp.asarray(factor, BF16)
    keys = k_ref[...]
    values = v_ref[...]
    grads = g_ref[...]
    product = (grads.astype(F32) * out_ref[...].astype(F32)).T
    dq = jnp.zeros(product.shape, F32)
    for head in range(width // HEAD):
        own_queries = only_head(queries, head)
        own_grads = only_head(grads, head)
        lse = lse_ref[head * HEAD : head * HEAD + 1, :]
        inner = jnp.sum(product[head * HEAD : (head + 1) * HEAD], 0, keepdims=True)
        probs = jnp.exp(dot_nt(keys, own_queries) - lse)
        prob_grad = dot_nt(values, own_grads)
        score_grad = (probs * (prob_grad - inner)).astype(BF16)
        dv_sum[...] += dot_nn(probs.astype(BF16), own_grads)
        dk_sum[...] += dot_nn(score_grad, own_queries)
        dq = dq + dot_tn(only_head(keys, head), score_grad)
    dq = (dq.T * factor).astype(BF16).astype(F32)
    here = pl.ds(pl.multiple_of(step * step_rows, ROW_TILE), step_rows)
    packed_ref[here, :width] = (dq * cos_ref[here, :] - partner(dq) * sin_ref[here, :]).astype(BF16)

    @pl.when(step == pl.num_programs(0) - 1)
    def _():
        dk = dk_sum[...].astype(BF16).astype(F32)
        packed_ref[:, width : 2 * width] = (
            dk * cos_ref[...] - partner(dk) * sin_ref[...]
        ).astype(BF16)
        packed_ref[:, 2 * width :] = dv_sum[...].astype(BF16)


def attend_back(queries, keys, values, grads, out, lse, cosine, sine, group):
    rows, local_width = queries.shape
    width = min(128, local_width)
    step = block_rows(rows, 512)
    q_spec = pl.BlockSpec((step, width), lambda i: (i, group))
    k_spec = pl.BlockSpec((rows, width), lambda i: (0, group))
    own_spec = pl.BlockSpec((step, width), lambda i: (i, 0))
    all_spec = pl.BlockSpec((rows, width), lambda i: (0, 0))
    return pl.pallas_call(
        attend_back_body,
        grid=(rows // step,),
        in_specs=[
            q_spec, k_spec, k_spec, own_spec, own_spec,
            pl.BlockSpec((width, step), lambda i: (0, i)),
            all_spec, all_spec,
        ],
        out_specs=pl.BlockSpec((rows, 3 * width), lambda i: (0, 0)),
        out_shape=jax.ShapeDtypeStruct((rows, 3 * width), BF16),
        scratch_shapes=[pltpu.VMEM((rows, width), F32)] * 2,
        compiler_params=pltpu.CompilerParams(vmem_limit_bytes=VMEM_BYTES),
        cost_estimate=pl.CostEstimate(
            flops=40 * rows * rows * width,
            bytes_accessed=20 * rows * width,
            transcendentals=rows * rows * width // HEAD,
        ),
        name="attend_back",
    )(queries, keys, values, grads, out, lse, cosine, sine)


def mlp_body(count, steps, blocks, units, *refs):
    x_pieces, c_pieces = refs[:count], refs[count : 2 * count]
    weights_ref = refs[2 * count]
    x_scratch, c_scratch, wo_ref = refs[-3:]
    results = refs[-3 - 4 - 2 * count : -3]
    wi_ref = weights_ref.at[:, : 2 * units]
    depth = wo_ref.shape[1]

    @pl.when(pl.program_id(0) == 0)
    def _():
        shard, share = depth // blocks, units // blocks
        rows = math.gcd(share, shard)
        wide = depth * rows // shard
        for block in range(blocks):
            for tall in range(share // rows):
                for at in range(shard // rows):
                    wo_ref[
                        pl.ds(block * share + tall * rows, rows), at * wide : (at + 1) * wide
                    ] = weights_ref[
                        pl.ds(block * shard + at * rows, rows),
                        2 * units + tall * wide : 2 * units + (tall + 1) * wide,
                    ]

    hidden_ref, gate_up_ref, x_ref, c_ref = results[:4]
    back_refs, out_refs = results[4 : 4 + count], results[4 + count :]
    x = take_piece(x_pieces, steps, x_scratch)
    cotangent = take_piece(c_pieces, steps, c_scratch)
    x_ref[...] = x
    c_ref[...] = cotangent
    gate_up = dot_nn(x, wi_ref[...])
    hidden_grad = dot_nt(cotangent, wo_ref[...])
    gate = gate_up[:, :units]
    up = gate_up[:, units:]
    share = 0.5 * (1.0 + lax.erf(gate * 2.0**-0.5))
    activated = gate * share
    slope = share + gate * jnp.exp(-0.5 * gate * gate) * (2.0 * math.pi) ** -0.5
    hidden = (activated * up).astype(BF16)
    hidden_ref[...] = hidden
    gate_grad = (hidden_grad * up * slope).astype(BF16)
    up_grad = (hidden_grad * activated).astype(BF16)
    both = jnp.concatenate([gate_grad, up_grad], 1)
    gate_up_ref[...] = both
    back = dot_nt(both, wi_ref[...]).astype(BF16)
    out = dot_nn(hidden, wo_ref[...]).astype(BF16)
    for at in range(count):

        @pl.when(pl.program_id(0) // steps == at)
        def _(at=at):
            back_refs[at][...] = back
            out_refs[at][...] = out


def fold_rows(values, shard):
    share, depth = values.shape
    rows = math.gcd(share, shard)
    tall, wide = share // rows, shard // rows
    return (
        values.reshape(tall, rows, wide, depth // wide)
        .transpose(2, 1, 0, 3)
        .reshape(shard, tall * depth // wide)
    )


def mlp(x_pieces, c_pieces, weights, units, blocks, length, before):
    count = len(x_pieces)
    rows, depth = x_pieces[0].shape
    step = block_rows(rows, 320)
    steps = rows // step
    total = count * rows
    first = count * steps if before else 0
    by_row = lambda columns: pl.BlockSpec((step, columns), lambda i: (i + first, 0))
    whole = lambda shape: pl.BlockSpec(shape, lambda i: (0, 0))
    pieces = piece_specs(count, steps, step, depth)
    results = pl.pallas_call(
        functools.partial(mlp_body, count, steps, blocks, units),
        grid=(count * steps,),
        in_specs=pieces
        + pieces
        + [whole(weights.shape)]
        + [pl.BlockSpec(memory_space=pl.ANY)] * len(before),
        out_specs=[by_row(units), by_row(2 * units), by_row(depth), by_row(depth)]
        + pieces
        + pieces,
        out_shape=[
            jax.ShapeDtypeStruct((length, columns), BF16)
            for columns in (units, 2 * units, depth, depth)
        ]
        + [jax.ShapeDtypeStruct((rows, depth), BF16)] * (2 * count),
        scratch_shapes=[pltpu.VMEM((step, depth), BF16)] * 2 + [pltpu.VMEM((units, depth), BF16)],
        input_output_aliases={2 * count + 1 + at: at for at in range(len(before))},
        compiler_params=pltpu.CompilerParams(vmem_limit_bytes=VMEM_BYTES),
        cost_estimate=pl.CostEstimate(
            flops=12 * total * depth * units,
            bytes_accessed=2 * total * (6 * depth + 3 * units) + 6 * depth * units,
            transcendentals=2 * total * units,
        ),
        name="mlp",
    )(*x_pieces, *c_pieces, weights, *before)
    return results[:4], results[4 : 4 + count], results[4 + count :]


def token_grad_body(blocks, groups, count, steps, *refs):
    packed = jnp.concatenate([ref[...] for ref in refs[:groups]], 1)
    results = refs[groups + 1 :]
    grad = reorder(dot_nt(packed, refs[groups][...]).astype(BF16), blocks)
    for at in range(count):

        @pl.when(pl.program_id(0) // steps == at)
        def _(at=at):
            results[at][...] = grad


def token_grad(packed, weights, blocks, count, positions, first):
    groups = len(packed)
    depth = weights.shape[0]
    columns = groups * packed[0].shape[1]
    step = block_rows(positions, 320)
    steps = positions // step
    total = count * positions
    return pl.pallas_call(
        functools.partial(token_grad_body, blocks, groups, count, steps),
        grid=(count * steps,),
        in_specs=[
            pl.BlockSpec((step, columns // groups), lambda i: (i + first * steps, 0))
        ] * groups
        + [pl.BlockSpec(weights.shape, lambda i: (0, 0))],
        out_specs=piece_specs(count, steps, step, depth),
        out_shape=[jax.ShapeDtypeStruct((positions, depth), BF16)] * count,
        compiler_params=pltpu.CompilerParams(vmem_limit_bytes=VMEM_BYTES),
        cost_estimate=pl.CostEstimate(
            flops=2 * total * depth * columns,
            bytes_accessed=2 * (total * depth + depth * columns + total * columns),
            transcendentals=0,
        ),
        name="token_grad",
    )(*packed, weights)


def local(seq_size, fsdp_size, activations, cotangent, gain_attn, w_qkv, w_attn_out, gain_mlp, w_in, w_mlp_out):
    _, positions, width = activations.shape
    shard = w_qkv.shape[0]
    ff_shard = w_mlp_out.shape[0]
    local_width = width // seq_size
    length = positions * seq_size
    half = seq_size // 2
    lanes = min(128, local_width)
    groups = local_width // lanes
    me = lax.axis_index("seq")
    row = lax.axis_index("fsdp")
    after = lax.optimization_barrier


    def swap(values, axis, size, offset):
        return lax.ppermute(values, axis, [(i, i ^ offset) for i in range(size)])

    def swap_seq(values, offset):
        return swap(values, "seq", seq_size, offset)

    def spread(values):
        pieces = [values]
        bit = 1
        while bit < half:
            pieces = pieces + [swap_seq(piece, bit) for piece in pieces]
            bit *= 2
        return pieces

    def gather_seq(values):
        return spread(values) + spread(swap_seq(values, half))

    def fold(pieces):
        pieces = list(pieces)
        while len(pieces) > 1:
            left = len(pieces) // 2
            got = [swap_seq(piece.astype(BF16), left) for piece in pieces[left:]]
            pieces = [kept.astype(F32) + other.astype(F32) for kept, other in zip(pieces, got)]
        return pieces[0].astype(F32)

    def far_sum(pieces):
        return swap_seq(fold(pieces).astype(BF16), half)

    def exchange_seq(pieces):
        return [pieces[0]] + [swap_seq(pieces[k], k) for k in range(1, seq_size)]

    def by_member(pieces):
        stacked = jnp.stack(pieces)
        return [
            lax.dynamic_index_in_dim(stacked, me ^ member, 0, keepdims=False)
            for member in range(seq_size)
        ]

    def double_fsdp(values, bit, joined=lambda got: got):
        other = joined(swap(values, "fsdp", fsdp_size, bit))
        high = (row & bit) != 0
        return jnp.concatenate(
            [jnp.where(high, other, values), jnp.where(high, values, other)], 0
        )

    def halve_fsdp(values, bit, joined=lambda got: got):
        size = values.shape[0] // 2
        mine = jnp.where((row & bit) != 0, size, 0)
        kept = lax.dynamic_slice(values, (mine, 0), (size, values.shape[1]))
        sent = lax.dynamic_slice(values, (size - mine, 0), (size, values.shape[1]))
        got = joined(swap(sent, "fsdp", fsdp_size, bit))
        return (kept.astype(F32) + got.astype(F32)).astype(BF16)

    def reduce_fsdp(values):
        return lax.psum_scatter(values, "fsdp", scatter_dimension=0, tiled=True)

    own_gain_attn = gain_attn.astype(F32)[:, None]
    own_gain_mlp = gain_mlp.astype(F32)[:, None]

    qkv_slice = jnp.concatenate(
        [
            lax.dynamic_slice(
                w_qkv, (0, part * width + me * local_width + group * lanes), (shard, lanes)
            )
            for group in range(groups)
            for part in range(3)
        ],
        1,
    )
    qkv_slice = (qkv_slice.astype(F32) * own_gain_attn).astype(BF16)
    attn_out_slice = lax.dynamic_slice(w_attn_out, (0, me * local_width), (shard, local_width))

    tokens = activations.reshape(positions, width).astype(F32)
    xhat, inverse = centred_stats(tokens)
    own_x = xhat.astype(BF16)
    far_x = swap_seq(own_x, half)
    near_x_pieces = spread(own_x)
    far_x_pieces = spread(far_x)
    own_cotangent = cotangent.reshape(positions, width)
    near_c_pieces = spread(own_cotangent)

    unit_share = -(-ff_shard // seq_size)
    unit_share = -(-unit_share // ROW_TILE) * ROW_TILE
    padding = unit_share * seq_size - ff_shard
    units = fsdp_size * unit_share
    mlp_out_slice = lax.dynamic_slice(
        jnp.pad(w_mlp_out, ((0, padding), (0, 0))), (me * unit_share, 0), (unit_share, width)
    )
    in_slice = jnp.pad(
        w_in.reshape(shard, 2 * fsdp_size, ff_shard), ((0, 0), (0, 0), (0, padding))
    )
    in_slice = lax.dynamic_slice(
        in_slice, (0, 0, me * unit_share), (shard, 2 * fsdp_size, unit_share)
    ).reshape(shard, 2 * units)
    in_slice = (in_slice.astype(F32) * own_gain_mlp).astype(BF16)
    def rotary_tables(device):
        lane = lax.broadcasted_iota(jnp.int32, (length, lanes), 1)
        at = lax.broadcasted_iota(jnp.int32, (length, lanes), 0)
        place = ((at // positions) ^ device) * positions + at % positions
        frequency = jnp.exp((lane % HALF).astype(F32) * (-2.0 * math.log(rope_base) / HEAD))
        angles = place.astype(F32) * frequency
        cosine = jnp.cos(angles)
        sine = jnp.sin(angles) * jnp.where(lane % HEAD < HALF, -1.0, 1.0)
        return cosine, sine

    bit = fsdp_size // 2
    qkv_weights, sections = qkv_slice, attn_out_slice
    while bit:
        join = lambda got: got
        if bit == 1:
            device, qkv_weights = after((me, qkv_weights))
            cosine, sine = rotary_tables(device)
            join = lambda got: after((got, cosine, sine))[0]
        doubled = double_fsdp(qkv_weights, bit, join)
        if bit < fsdp_size // 2:
            sections, qkv_weights = after((sections, qkv_weights))
            sections = double_fsdp(sections, 2 * bit)
        qkv_weights = doubled
        bit //= 2
    begun = qkv_heads(near_x_pieces, qkv_weights, cosine, sine, fsdp_size, [])
    sections = double_fsdp(
        after((sections, qkv_weights))[0], 1, lambda got: after((got, begun))[0]
    )
    sections = jnp.concatenate(
        [sections[block * shard : (block + 1) * shard] for block in bit_reversed(fsdp_size)], 0
    )
    mlp_slice = jnp.concatenate([in_slice, fold_rows(mlp_out_slice, shard)], 1)
    mlp_weights = lax.all_gather(after((mlp_slice, qkv_weights))[0], "fsdp", axis=0, tiled=True)
    far_sections = swap_seq(after((sections, far_x))[0], half)
    far_c_pieces = spread(swap_seq(after((own_cotangent, far_sections))[0], half))

    queries, keys, values, x_all = qkv_heads(
        far_x_pieces, qkv_weights, cosine, sine, fsdp_size, begun
    )

    def row_pieces(array):
        return [array[k * positions : (k + 1) * positions] for k in range(seq_size)]

    heads = [attend(after((queries, far_sections))[0], keys, values, 0)]
    group_pieces = [exchange_seq(row_pieces(heads[0][0]))]
    for group in range(1, groups):
        heads.append(attend(after((queries, far_c_pieces[0], heads[0]))[0], keys, values, group))
        group_pieces.append(exchange_seq(row_pieces(heads[group][0])))
    attn_out_full = jnp.concatenate(by_member(spread(sections) + spread(far_sections)), 1)
    attended_pieces = [jnp.concatenate(pieces, 1) for pieces in zip(*group_pieces)]
    attn_out_ordered = jnp.concatenate(
        [
            lax.dynamic_slice(
                attn_out_full, ((me ^ member) * local_width, 0), (local_width, width)
            )
            for member in range(seq_size)
        ],
        0,
    )
    attended = jnp.concatenate(attended_pieces, 1)
    mixed = tokens + dot_nn(attended, attn_out_ordered)
    xhat_mlp, inverse_mlp = centred_stats(mixed)
    own_x_mlp = xhat_mlp.astype(BF16)
    far_x_mlp = swap_seq(own_x_mlp, half)
    begun, near_back, near_out = mlp(
        spread(own_x_mlp), near_c_pieces, mlp_weights, units, fsdp_size, length, []
    )
    far_x_mlp, begun = after((far_x_mlp, begun))
    (hidden, gate_up_grad, x_mlp_all, cotangent_all), far_back, far_out = mlp(
        spread(far_x_mlp), far_c_pieces, mlp_weights, units, fsdp_size, length, begun
    )
    back_far = far_sum(far_back)
    back_near = fold(near_back)
    grad_mlp_out = dot_tn(hidden, cotangent_all).astype(BF16)
    grad_in = dot_tn(x_mlp_all, gate_up_grad).astype(BF16)
    back_far, grad_mlp_out, grad_in = after((back_far, grad_mlp_out, grad_in))

    mixed_grad = own_cotangent.astype(F32) + norm_backward(
        back_near + back_far.astype(F32), xhat_mlp, inverse_mlp
    )
    mixed_low = mixed_grad.astype(BF16)
    attended_grad = dot_nt(mixed_low, attn_out_ordered).astype(BF16)
    grads = []
    for group in range(groups):
        columns = [k * local_width + group * lanes for k in range(seq_size)]
        pieces = [attended_grad[:, start : start + lanes] for start in columns]
        grads.append(jnp.concatenate(exchange_seq(pieces), 0))
    attended_natural = jnp.concatenate(by_member(attended_pieces), 1)
    grad_attn_out = dot_tn(reorder(attended_natural, fsdp_size), mixed_low).astype(BF16)
    grads[0], grad_attn_out = after((grads[0], grad_attn_out))
    column_pieces = [
        lax.dynamic_slice(grad_attn_out, (0, (me ^ k) * local_width), (width, local_width))
        for k in range(seq_size)
    ]
    near_attn_out = fold(column_pieces[:half])
    far_attn_out = fold(column_pieces[half:]).astype(BF16)
    sum_near_out = fold(near_out)
    sum_far_out = fold(far_out).astype(BF16)
    grads[0], sum_far_out, far_attn_out = after((grads[0], sum_far_out, far_attn_out))
    sum_far_out = swap_seq(sum_far_out, half)
    far_attn_out = swap_seq(far_attn_out, half)

    def back_of(group):
        out, lse = heads[group]
        return attend_back(queries, keys, values, grads[group], out, lse, cosine, sine, group)

    packed = [back_of(0)]
    packed[0], sum_far_out, far_attn_out = after((packed[0], sum_far_out, far_attn_out))
    output = (mixed + (sum_near_out + sum_far_out.astype(F32))).astype(BF16)
    grad_attn_out = (near_attn_out + far_attn_out.astype(F32)).astype(BF16)
    first_grads = jnp.concatenate(
        [dot_tn(x_all, packed[0]).astype(BF16), grad_attn_out], 1
    )
    sum_in = reduce_fsdp(grad_in)
    sum_mlp_out = reduce_fsdp(after((grad_mlp_out, grad_in))[0])
    for group in range(1, groups):
        grads[group], output, _, sum_in = after(
            (grads[group], output, first_grads, sum_in)
        )
        packed.append(back_of(group))
    reduced = [halve_fsdp(first_grads, 1, lambda got: after((got, packed[-1]))[0])]

    later_bits = [1 << at for at in range(1, fsdp_size.bit_length() - 1)]
    chains = [later_bits] + [[0, 1] + later_bits] * (groups - 1)
    far_grads = fold(token_grad(packed, qkv_weights, fsdp_size, half, positions, half))
    far_grads = far_grads.astype(BF16)
    reduced = reduced + [dot_tn(x_all, section).astype(BF16) for section in packed[1:]]
    cuts = [0, positions // 4, positions // 2, positions]
    near_grads, far_parts = None, None
    for stage in range(max(len(chain) for chain in chains)):
        if stage == 1:
            far_parts = [
                swap_seq(far_grads[start:end], half) for start, end in zip(cuts, cuts[1:])
            ]
            near_grads = token_grad(packed, qkv_weights, fsdp_size, half, positions, 0)
        if stage == 2:
            near_grads = fold(near_grads)
        reduced = [
            halve_fsdp(section, chain[stage])
            if stage < len(chain) and chain[stage]
            else section
            for section, chain in zip(reduced, chains)
        ]
        if stage == 0:
            reduced, far_grads, packed, sum_mlp_out = after(
                (reduced, far_grads, packed, sum_mlp_out)
            )
        if stage == 1:
            reduced, near_grads, far_parts[0] = after((reduced, near_grads, far_parts[0]))
        if stage == 2:
            reduced, near_grads, far_parts[1] = after((reduced, near_grads, far_parts[1]))
    if not isinstance(near_grads, jax.Array):
        near_grads = fold(near_grads)
    reduced = jnp.concatenate(reduced, 1)
    far_reduced = swap_seq(reduced, half)
    far_reduced, far_parts = after((far_reduced, far_parts))
    sum_mlp_out = after((sum_mlp_out, far_parts[0]))[0]
    normed_grad = jnp.concatenate(far_parts, 0).astype(F32) + near_grads
    d_input = (mixed_grad + norm_backward(normed_grad, xhat, inverse)).astype(BF16)

    in_pieces = by_member(gather_seq(sum_in))
    all_in = jnp.concatenate(
        [piece.reshape(shard, 2 * fsdp_size, unit_share) for piece in in_pieces], 2
    )
    all_in = all_in[:, :, :ff_shard].reshape(shard, -1).astype(F32)
    all_mlp_out = jnp.concatenate(by_member(gather_seq(sum_mlp_out)), 0)[:ff_shard].astype(F32)
    pieces = by_member(spread(reduced) + spread(far_reduced))
    section = 3 * lanes
    all_attn_out = jnp.concatenate(
        [piece[:, section : section + local_width] for piece in pieces], 1
    ).astype(F32)
    starts = [0] + [section * group + local_width for group in range(1, groups)]
    all_qkv = jnp.concatenate(
        [
            piece[:, start + part * lanes : start + (part + 1) * lanes]
            for part in range(3)
            for piece in pieces
            for start in starts
        ],
        1,
    ).astype(F32)
    grad_gain_attn = jnp.sum(all_qkv * w_qkv.astype(F32), 1)
    grad_gain_mlp = jnp.sum(all_in * w_in.astype(F32), 1)
    return (
        output.reshape(activations.shape),
        d_input.reshape(activations.shape),
        grad_gain_attn,
        grad_gain_mlp,
        all_qkv * own_gain_attn,
        all_attn_out,
        all_in * own_gain_mlp,
        all_mlp_out,
    )


def solution(mesh):
    in_specs = (
        P("fsdp", "seq", None),
        P("fsdp", "seq", None),
        P("fsdp"),
        P("fsdp", None),
        P("fsdp", None),
        P("fsdp"),
        P("fsdp", None),
        P("fsdp", None),
    )
    out_specs = (
        P("fsdp", "seq", None),
        P("fsdp", "seq", None),
        P("fsdp"),
        P("fsdp"),
        P("fsdp", None),
        P("fsdp", None),
        P("fsdp", None),
        P("fsdp", None),
    )
    body = functools.partial(local, mesh.shape["seq"], mesh.shape["fsdp"])
    return jax.shard_map(body, mesh=mesh, in_specs=in_specs, out_specs=out_specs, check_vma=False)
```

```python
import functools
import math

import jax
import jax.numpy as jnp
from jax import lax
from jax.experimental import pallas as pl
from jax.experimental.pallas import tpu as pltpu
from jax.sharding import PartitionSpec as P

HEADS = 16
HEAD = 64
HALF = HEAD // 2
ROW_TILE = 16
BF16 = jnp.bfloat16
F32 = jnp.float32

eps = 1e-05
rope_base = 160000.0
VMEM_BYTES = 60 << 20


def dot_nn(a, b):
    return lax.dot_general(a, b, (((1,), (0,)), ((), ())), preferred_element_type=F32)


def dot_nt(a, b):
    return lax.dot_general(a, b, (((1,), (1,)), ((), ())), preferred_element_type=F32)


def dot_tn(a, b):
    return lax.dot_general(a, b, (((0,), (0,)), ((), ())), preferred_element_type=F32)


def block_rows(rows, wanted):
    best = rows
    for size in range(ROW_TILE, min(rows, wanted) + 1, ROW_TILE):
        if rows % size == 0:
            best = size
    return best


def centred_stats(values):
    average = jnp.mean(values, -1, keepdims=True)
    centred = values - average
    inverse = lax.rsqrt(jnp.mean(centred * centred, -1, keepdims=True) + eps)
    return centred * inverse, inverse


def norm_backward(grad, xhat, inverse):
    return inverse * (
        grad
        - jnp.mean(grad, -1, keepdims=True)
        - xhat * jnp.mean(grad * xhat, -1, keepdims=True)
    )


def partner(values):
    width = values.shape[-1]
    if width % 128:
        return jnp.concatenate([values[:, HALF:], values[:, :HALF]], 1)
    lane = lax.broadcasted_iota(jnp.int32, values.shape, 1)
    return jnp.where(
        lane % HEAD < HALF,
        pltpu.roll(values, width - HALF, 1),
        pltpu.roll(values, HALF, 1),
    )


def head_of_lane(shape):
    return lax.broadcasted_iota(jnp.int32, shape, 1) // HEAD


def only_head(values, head):
    return jnp.where(head_of_lane(values.shape) == head, values, jnp.zeros_like(values))


def take_piece(piece_refs, steps, scratch):
    for at, ref in enumerate(piece_refs):

        @pl.when(pl.program_id(0) // steps == at)
        def _(ref=ref):
            scratch[...] = ref[...]

    return scratch[...]


def piece_specs(count, steps, rows, columns):
    return [
        pl.BlockSpec(
            (rows, columns), lambda i, at=at: (jnp.clip(i - at * steps, 0, steps - 1), 0)
        )
        for at in range(count)
    ]


def bit_reversed(count):
    order = [0]
    while len(order) < count:
        order = [2 * at for at in order] + [2 * at + 1 for at in order]
    return order


def reorder(values, blocks):
    size = values.shape[1] // blocks
    return jnp.concatenate(
        [values[:, at * size : (at + 1) * size] for at in bit_reversed(blocks)], 1
    )


def qkv_body(blocks, count, steps, *refs):
    pieces, (w_ref, cos_ref, sin_ref) = refs[:count], refs[count : count + 3]
    q_ref, k_ref, v_ref, x_ref, scratch = refs[-5:]
    width = q_ref.shape[1]
    x = reorder(take_piece(pieces, steps, scratch), blocks)
    x_ref[...] = x
    packed = dot_nn(x, w_ref[...])
    cosine = cos_ref[...]
    sine = sin_ref[...]
    lanes = cosine.shape[1]
    for group in range(width // lanes):
        here = slice(group * lanes, (group + 1) * lanes)
        for at, ref in enumerate((q_ref, k_ref, v_ref)):
            start = (3 * group + at) * lanes
            part = packed[:, start : start + lanes]
            if at < 2:
                part = part * cosine + partner(part) * sine
            ref[:, here] = part.astype(BF16)


def qkv_heads(pieces, weights, cosine, sine, blocks, before):
    count = len(pieces)
    rows, depth = pieces[0].shape
    width = weights.shape[1] // 3
    step = block_rows(rows, 320)
    steps = rows // step
    length, table = cosine.shape
    first = count * steps if before else 0
    by_row = lambda columns: pl.BlockSpec((step, columns), lambda i: (i + first, 0))
    total = count * rows
    return pl.pallas_call(
        functools.partial(qkv_body, blocks, count, steps),
        grid=(count * steps,),
        in_specs=piece_specs(count, steps, step, depth)
        + [pl.BlockSpec(weights.shape, lambda i: (0, 0)), by_row(table), by_row(table)]
        + [pl.BlockSpec(memory_space=pl.ANY)] * len(before),
        out_specs=[by_row(width)] * 3 + [by_row(depth)],
        out_shape=[jax.ShapeDtypeStruct((length, width), BF16)] * 3
        + [jax.ShapeDtypeStruct((length, depth), BF16)],
        scratch_shapes=[pltpu.VMEM((step, depth), BF16)],
        input_output_aliases={count + 3 + at: at for at in range(len(before))},
        compiler_params=pltpu.CompilerParams(vmem_limit_bytes=VMEM_BYTES),
        cost_estimate=pl.CostEstimate(
            flops=6 * total * depth * width,
            bytes_accessed=2 * (2 * total * depth + 3 * depth * width + 3 * total * width),
            transcendentals=0,
        ),
        name="qkv_rope",
    )(*pieces, weights, cosine, sine, *before)


def attend_body(q_ref, k_ref, v_ref, out_ref, lse_ref):
    width = q_ref.shape[1]
    heads = width // HEAD
    queries = q_ref[...] * jnp.asarray(HEAD**-0.5, BF16)
    keys = k_ref[...]
    values = v_ref[...]
    outs, totals, peaks = [], [], []
    for head in range(heads):
        scores = dot_nt(keys, only_head(queries, head))
        peak = jnp.max(scores, 0, keepdims=True)
        exponent = jnp.exp(scores - peak)
        low = exponent.astype(BF16)
        if heads == 2:
            own = head_of_lane(values.shape) == head
            both = dot_tn(jnp.where(own, values, jnp.ones_like(values)), low)
            outs.append(both[head * HEAD : (head + 1) * HEAD])
            totals.append(both[(1 - head) * HEAD : (2 - head) * HEAD])
        else:
            outs.append(dot_tn(values, low)[head * HEAD : (head + 1) * HEAD])
            totals.append(
                jnp.broadcast_to(jnp.sum(exponent, 0, keepdims=True), outs[-1].shape)
            )
        peaks.append(jnp.broadcast_to(peak, outs[-1].shape))
    total = jnp.concatenate(totals, 0)
    out_ref[...] = (jnp.concatenate(outs, 0) / total).T.astype(BF16)
    lse_ref[...] = jnp.concatenate(peaks, 0) + jnp.log(total)


def attend(queries, keys, values, group):
    rows, local_width = queries.shape
    width = min(128, local_width)
    step = rows // 2
    q_spec = pl.BlockSpec((step, width), lambda i: (i, group))
    k_spec = pl.BlockSpec((rows, width), lambda i: (0, group))
    return pl.pallas_call(
        attend_body,
        grid=(rows // step,),
        in_specs=[q_spec, k_spec, k_spec],
        out_specs=[
            pl.BlockSpec((step, width), lambda i: (i, 0)),
            pl.BlockSpec((width, step), lambda i: (0, i)),
        ],
        out_shape=[
            jax.ShapeDtypeStruct((rows, width), BF16),
            jax.ShapeDtypeStruct((width, rows), F32),
        ],
        compiler_params=pltpu.CompilerParams(vmem_limit_bytes=VMEM_BYTES),
        cost_estimate=pl.CostEstimate(
            flops=16 * rows * rows * width,
            bytes_accessed=8 * rows * width,
            transcendentals=rows * rows * width // HEAD,
        ),
        name="attend",
    )(queries, keys, values)


def attend_back_body(
    q_ref, k_ref, v_ref, g_ref, out_ref, lse_ref, cos_ref, sin_ref, packed_ref, dk_sum, dv_sum
):
    step_rows, width = q_ref.shape
    step = pl.program_id(0)

    @pl.when(step == 0)
    def _():
        dk_sum[...] = jnp.zeros_like(dk_sum)
        dv_sum[...] = jnp.zeros_like(dv_sum)

    factor = HEAD**-0.5
    queries = q_ref[...] * jnp.asarray(factor, BF16)
    keys = k_ref[...]
    values = v_ref[...]
    grads = g_ref[...]
    product = (grads.astype(F32) * out_ref[...].astype(F32)).T
    dq = jnp.zeros(product.shape, F32)
    for head in range(width // HEAD):
        own_queries = only_head(queries, head)
        own_grads = only_head(grads, head)
        lse = lse_ref[head * HEAD : head * HEAD + 1, :]
        inner = jnp.sum(product[head * HEAD : (head + 1) * HEAD], 0, keepdims=True)
        probs = jnp.exp(dot_nt(keys, own_queries) - lse)
        prob_grad = dot_nt(values, own_grads)
        score_grad = (probs * (prob_grad - inner)).astype(BF16)
        dv_sum[...] += dot_nn(probs.astype(BF16), own_grads)
        dk_sum[...] += dot_nn(score_grad, own_queries)
        dq = dq + dot_tn(only_head(keys, head), score_grad)
    dq = (dq.T * factor).astype(BF16).astype(F32)
    here = pl.ds(pl.multiple_of(step * step_rows, ROW_TILE), step_rows)
    packed_ref[here, :width] = (dq * cos_ref[here, :] - partner(dq) * sin_ref[here, :]).astype(BF16)

    @pl.when(step == pl.num_programs(0) - 1)
    def _():
        dk = dk_sum[...].astype(BF16).astype(F32)
        packed_ref[:, width : 2 * width] = (
            dk * cos_ref[...] - partner(dk) * sin_ref[...]
        ).astype(BF16)
        packed_ref[:, 2 * width :] = dv_sum[...].astype(BF16)


def attend_back(queries, keys, values, grads, out, lse, cosine, sine, group):
    rows, local_width = queries.shape
    width = min(128, local_width)
    step = block_rows(rows, 512)
    q_spec = pl.BlockSpec((step, width), lambda i: (i, group))
    k_spec = pl.BlockSpec((rows, width), lambda i: (0, group))
    own_spec = pl.BlockSpec((step, width), lambda i: (i, 0))
    all_spec = pl.BlockSpec((rows, width), lambda i: (0, 0))
    return pl.pallas_call(
        attend_back_body,
        grid=(rows // step,),
        in_specs=[
            q_spec, k_spec, k_spec, own_spec, own_spec,
            pl.BlockSpec((width, step), lambda i: (0, i)),
            all_spec, all_spec,
        ],
        out_specs=pl.BlockSpec((rows, 3 * width), lambda i: (0, 0)),
        out_shape=jax.ShapeDtypeStruct((rows, 3 * width), BF16),
        scratch_shapes=[pltpu.VMEM((rows, width), F32)] * 2,
        compiler_params=pltpu.CompilerParams(vmem_limit_bytes=VMEM_BYTES),
        cost_estimate=pl.CostEstimate(
            flops=40 * rows * rows * width,
            bytes_accessed=20 * rows * width,
            transcendentals=rows * rows * width // HEAD,
        ),
        name="attend_back",
    )(queries, keys, values, grads, out, lse, cosine, sine)


def mlp_body(count, steps, blocks, units, *refs):
    x_pieces, c_pieces = refs[:count], refs[count : 2 * count]
    weights_ref = refs[2 * count]
    x_scratch, c_scratch, wo_ref = refs[-3:]
    results = refs[-3 - 4 - 2 * count : -3]
    wi_ref = weights_ref.at[:, : 2 * units]
    depth = wo_ref.shape[1]

    @pl.when(pl.program_id(0) == 0)
    def _():
        shard, share = depth // blocks, units // blocks
        rows = math.gcd(share, shard)
        wide = depth * rows // shard
        for block in range(blocks):
            for tall in range(share // rows):
                for at in range(shard // rows):
                    wo_ref[
                        pl.ds(block * share + tall * rows, rows), at * wide : (at + 1) * wide
                    ] = weights_ref[
                        pl.ds(block * shard + at * rows, rows),
                        2 * units + tall * wide : 2 * units + (tall + 1) * wide,
                    ]

    hidden_ref, gate_up_ref, x_ref, c_ref = results[:4]
    back_refs, out_refs = results[4 : 4 + count], results[4 + count :]
    x = take_piece(x_pieces, steps, x_scratch)
    cotangent = take_piece(c_pieces, steps, c_scratch)
    x_ref[...] = x
    c_ref[...] = cotangent
    gate_up = dot_nn(x, wi_ref[...])
    hidden_grad = dot_nt(cotangent, wo_ref[...])
    gate = gate_up[:, :units]
    up = gate_up[:, units:]
    share = 0.5 * (1.0 + lax.erf(gate * 2.0**-0.5))
    activated = gate * share
    slope = share + gate * jnp.exp(-0.5 * gate * gate) * (2.0 * math.pi) ** -0.5
    hidden = (activated * up).astype(BF16)
    hidden_ref[...] = hidden
    gate_grad = (hidden_grad * up * slope).astype(BF16)
    up_grad = (hidden_grad * activated).astype(BF16)
    both = jnp.concatenate([gate_grad, up_grad], 1)
    gate_up_ref[...] = both
    back = dot_nt(both, wi_ref[...]).astype(BF16)
    out = dot_nn(hidden, wo_ref[...]).astype(BF16)
    for at in range(count):

        @pl.when(pl.program_id(0) // steps == at)
        def _(at=at):
            back_refs[at][...] = back
            out_refs[at][...] = out


def fold_rows(values, shard):
    share, depth = values.shape
    rows = math.gcd(share, shard)
    tall, wide = share // rows, shard // rows
    return (
        values.reshape(tall, rows, wide, depth // wide)
        .transpose(2, 1, 0, 3)
        .reshape(shard, tall * depth // wide)
    )


def mlp(x_pieces, c_pieces, weights, units, blocks, length, before):
    count = len(x_pieces)
    rows, depth = x_pieces[0].shape
    step = block_rows(rows, 320)
    steps = rows // step
    total = count * rows
    first = count * steps if before else 0
    by_row = lambda columns: pl.BlockSpec((step, columns), lambda i: (i + first, 0))
    whole = lambda shape: pl.BlockSpec(shape, lambda i: (0, 0))
    pieces = piece_specs(count, steps, step, depth)
    results = pl.pallas_call(
        functools.partial(mlp_body, count, steps, blocks, units),
        grid=(count * steps,),
        in_specs=pieces
        + pieces
        + [whole(weights.shape)]
        + [pl.BlockSpec(memory_space=pl.ANY)] * len(before),
        out_specs=[by_row(units), by_row(2 * units), by_row(depth), by_row(depth)]
        + pieces
        + pieces,
        out_shape=[
            jax.ShapeDtypeStruct((length, columns), BF16)
            for columns in (units, 2 * units, depth, depth)
        ]
        + [jax.ShapeDtypeStruct((rows, depth), BF16)] * (2 * count),
        scratch_shapes=[pltpu.VMEM((step, depth), BF16)] * 2 + [pltpu.VMEM((units, depth), BF16)],
        input_output_aliases={2 * count + 1 + at: at for at in range(len(before))},
        compiler_params=pltpu.CompilerParams(vmem_limit_bytes=VMEM_BYTES),
        cost_estimate=pl.CostEstimate(
            flops=12 * total * depth * units,
            bytes_accessed=2 * total * (6 * depth + 3 * units) + 6 * depth * units,
            transcendentals=2 * total * units,
        ),
        name="mlp",
    )(*x_pieces, *c_pieces, weights, *before)
    return results[:4], results[4 : 4 + count], results[4 + count :]


def token_grad_body(blocks, groups, count, steps, *refs):
    packed = jnp.concatenate([ref[...] for ref in refs[:groups]], 1)
    results = refs[groups + 1 :]
    grad = reorder(dot_nt(packed, refs[groups][...]).astype(BF16), blocks)
    for at in range(count):

        @pl.when(pl.program_id(0) // steps == at)
        def _(at=at):
            results[at][...] = grad


def token_grad(packed, weights, blocks, count, positions, first):
    groups = len(packed)
    depth = weights.shape[0]
    columns = groups * packed[0].shape[1]
    step = block_rows(positions, 320)
    steps = positions // step
    total = count * positions
    return pl.pallas_call(
        functools.partial(token_grad_body, blocks, groups, count, steps),
        grid=(count * steps,),
        in_specs=[
            pl.BlockSpec((step, columns // groups), lambda i: (i + first * steps, 0))
        ] * groups
        + [pl.BlockSpec(weights.shape, lambda i: (0, 0))],
        out_specs=piece_specs(count, steps, step, depth),
        out_shape=[jax.ShapeDtypeStruct((positions, depth), BF16)] * count,
        compiler_params=pltpu.CompilerParams(vmem_limit_bytes=VMEM_BYTES),
        cost_estimate=pl.CostEstimate(
            flops=2 * total * depth * columns,
            bytes_accessed=2 * (total * depth + depth * columns + total * columns),
            transcendentals=0,
        ),
        name="token_grad",
    )(*packed, weights)


def local(seq_size, fsdp_size, activations, cotangent, gain_attn, w_qkv, w_attn_out, gain_mlp, w_in, w_mlp_out):
    _, positions, width = activations.shape
    shard = w_qkv.shape[0]
    ff_shard = w_mlp_out.shape[0]
    local_width = width // seq_size
    length = positions * seq_size
    half = seq_size // 2
    lanes = min(128, local_width)
    groups = local_width // lanes
    me = lax.axis_index("seq")
    row = lax.axis_index("fsdp")
    after = lax.optimization_barrier


    def swap(values, axis, size, offset):
        return lax.ppermute(values, axis, [(i, i ^ offset) for i in range(size)])

    def swap_seq(values, offset):
        return swap(values, "seq", seq_size, offset)

    def spread(values):
        pieces = [values]
        bit = 1
        while bit < half:
            pieces = pieces + [swap_seq(piece, bit) for piece in pieces]
            bit *= 2
        return pieces

    def gather_seq(values):
        return spread(values) + spread(swap_seq(values, half))

    def fold(pieces):
        pieces = list(pieces)
        while len(pieces) > 1:
            left = len(pieces) // 2
            got = [swap_seq(piece.astype(BF16), left) for piece in pieces[left:]]
            pieces = [kept.astype(F32) + other.astype(F32) for kept, other in zip(pieces, got)]
        return pieces[0].astype(F32)

    def far_sum(pieces):
        return swap_seq(fold(pieces).astype(BF16), half)

    def exchange_seq(pieces):
        return [pieces[0]] + [swap_seq(pieces[k], k) for k in range(1, seq_size)]

    def by_member(pieces):
        stacked = jnp.stack(pieces)
        return [
            lax.dynamic_index_in_dim(stacked, me ^ member, 0, keepdims=False)
            for member in range(seq_size)
        ]

    def double_fsdp(values, bit, joined=lambda got: got):
        other = joined(swap(values, "fsdp", fsdp_size, bit))
        high = (row & bit) != 0
        return jnp.concatenate(
            [jnp.where(high, other, values), jnp.where(high, values, other)], 0
        )

    def halve_fsdp(values, bit, joined=lambda got: got):
        size = values.shape[0] // 2
        mine = jnp.where((row & bit) != 0, size, 0)
        kept = lax.dynamic_slice(values, (mine, 0), (size, values.shape[1]))
        sent = lax.dynamic_slice(values, (size - mine, 0), (size, values.shape[1]))
        got = joined(swap(sent, "fsdp", fsdp_size, bit))
        return (kept.astype(F32) + got.astype(F32)).astype(BF16)

    def reduce_fsdp(values):
        return lax.psum_scatter(values, "fsdp", scatter_dimension=0, tiled=True)

    own_gain_attn = gain_attn.astype(F32)[:, None]
    own_gain_mlp = gain_mlp.astype(F32)[:, None]

    qkv_slice = jnp.concatenate(
        [
            lax.dynamic_slice(
                w_qkv, (0, part * width + me * local_width + group * lanes), (shard, lanes)
            )
            for group in range(groups)
            for part in range(3)
        ],
        1,
    )
    qkv_slice = (qkv_slice.astype(F32) * own_gain_attn).astype(BF16)
    attn_out_slice = lax.dynamic_slice(w_attn_out, (0, me * local_width), (shard, local_width))

    tokens = activations.reshape(positions, width).astype(F32)
    xhat, inverse = centred_stats(tokens)
    own_x = xhat.astype(BF16)
    far_x = swap_seq(own_x, half)
    near_x_pieces = spread(own_x)
    far_x_pieces = spread(far_x)
    own_cotangent = cotangent.reshape(positions, width)
    near_c_pieces = spread(own_cotangent)

    unit_share = -(-ff_shard // seq_size)
    unit_share = -(-unit_share // ROW_TILE) * ROW_TILE
    padding = unit_share * seq_size - ff_shard
    units = fsdp_size * unit_share
    mlp_out_slice = lax.dynamic_slice(
        jnp.pad(w_mlp_out, ((0, padding), (0, 0))), (me * unit_share, 0), (unit_share, width)
    )
    in_slice = jnp.pad(
        w_in.reshape(shard, 2 * fsdp_size, ff_shard), ((0, 0), (0, 0), (0, padding))
    )
    in_slice = lax.dynamic_slice(
        in_slice, (0, 0, me * unit_share), (shard, 2 * fsdp_size, unit_share)
    ).reshape(shard, 2 * units)
    in_slice = (in_slice.astype(F32) * own_gain_mlp).astype(BF16)
    def rotary_tables(device):
        lane = lax.broadcasted_iota(jnp.int32, (length, lanes), 1)
        at = lax.broadcasted_iota(jnp.int32, (length, lanes), 0)
        place = ((at // positions) ^ device) * positions + at % positions
        frequency = jnp.exp((lane % HALF).astype(F32) * (-2.0 * math.log(rope_base) / HEAD))
        angles = place.astype(F32) * frequency
        cosine = jnp.cos(angles)
        sine = jnp.sin(angles) * jnp.where(lane % HEAD < HALF, -1.0, 1.0)
        return cosine, sine

    bit = fsdp_size // 2
    qkv_weights, sections = qkv_slice, attn_out_slice
    while bit:
        join = lambda got: got
        if bit == 1:
            device, qkv_weights = after((me, qkv_weights))
            cosine, sine = rotary_tables(device)
            join = lambda got: after((got, cosine, sine))[0]
        doubled = double_fsdp(qkv_weights, bit, join)
        if bit < fsdp_size // 2:
            sections, qkv_weights = after((sections, qkv_weights))
            sections = double_fsdp(sections, 2 * bit)
        qkv_weights = doubled
        bit //= 2
    begun = qkv_heads(near_x_pieces, qkv_weights, cosine, sine, fsdp_size, [])
    sections = double_fsdp(
        after((sections, qkv_weights))[0], 1, lambda got: after((got, begun))[0]
    )
    sections = jnp.concatenate(
        [sections[block * shard : (block + 1) * shard] for block in bit_reversed(fsdp_size)], 0
    )
    mlp_slice = jnp.concatenate([in_slice, fold_rows(mlp_out_slice, shard)], 1)
    mlp_weights = lax.all_gather(after((mlp_slice, qkv_weights))[0], "fsdp", axis=0, tiled=True)
    far_sections = swap_seq(after((sections, far_x))[0], half)
    far_c_pieces = spread(swap_seq(after((own_cotangent, far_x))[0], half))

    queries, keys, values, x_all = qkv_heads(
        far_x_pieces, qkv_weights, cosine, sine, fsdp_size, begun
    )

    def row_pieces(array):
        return [array[k * positions : (k + 1) * positions] for k in range(seq_size)]

    heads = [attend(queries, keys, values, 0)]
    group_pieces = [exchange_seq(row_pieces(heads[0][0]))]
    for group in range(1, groups):
        late_queries, _, far_sections, _ = after(
            (queries, far_c_pieces[0], far_sections, heads[0])
        )
        heads.append(attend(late_queries, keys, values, group))
        group_pieces.append(exchange_seq(row_pieces(heads[group][0])))
    attn_out_full = jnp.concatenate(by_member(spread(sections) + spread(far_sections)), 1)
    attended_pieces = [jnp.concatenate(pieces, 1) for pieces in zip(*group_pieces)]
    attn_out_ordered = jnp.concatenate(
        [
            lax.dynamic_slice(
                attn_out_full, ((me ^ member) * local_width, 0), (local_width, width)
            )
            for member in range(seq_size)
        ],
        0,
    )
    attended = jnp.concatenate(attended_pieces, 1)
    mixed = tokens + dot_nn(attended, attn_out_ordered)
    xhat_mlp, inverse_mlp = centred_stats(mixed)
    own_x_mlp = xhat_mlp.astype(BF16)
    far_x_mlp = swap_seq(own_x_mlp, half)
    begun, near_back, near_out = mlp(
        spread(own_x_mlp), near_c_pieces, mlp_weights, units, fsdp_size, length, []
    )
    far_x_mlp, begun = after((far_x_mlp, begun))
    (hidden, gate_up_grad, x_mlp_all, cotangent_all), far_back, far_out = mlp(
        spread(far_x_mlp), far_c_pieces, mlp_weights, units, fsdp_size, length, begun
    )
    back_far = far_sum(far_back)
    back_near = fold(near_back)
    grad_mlp_out = dot_tn(hidden, cotangent_all).astype(BF16)
    grad_in = dot_tn(x_mlp_all, gate_up_grad).astype(BF16)
    back_far, grad_mlp_out, grad_in = after((back_far, grad_mlp_out, grad_in))

    mixed_grad = own_cotangent.astype(F32) + norm_backward(
        back_near + back_far.astype(F32), xhat_mlp, inverse_mlp
    )
    mixed_low = mixed_grad.astype(BF16)
    attended_grad = dot_nt(mixed_low, attn_out_ordered).astype(BF16)
    grads = []
    for group in range(groups):
        columns = [k * local_width + group * lanes for k in range(seq_size)]
        pieces = [attended_grad[:, start : start + lanes] for start in columns]
        grads.append(jnp.concatenate(exchange_seq(pieces), 0))
    attended_natural = jnp.concatenate(by_member(attended_pieces), 1)
    grad_attn_out = dot_tn(reorder(attended_natural, fsdp_size), mixed_low).astype(BF16)
    grads[0], grad_attn_out = after((grads[0], grad_attn_out))
    column_pieces = [
        lax.dynamic_slice(grad_attn_out, (0, (me ^ k) * local_width), (width, local_width))
        for k in range(seq_size)
    ]
    near_attn_out = fold(column_pieces[:half])
    far_attn_out = fold(column_pieces[half:]).astype(BF16)
    sum_near_out = fold(near_out)
    sum_far_out = fold(far_out).astype(BF16)
    grads[0], sum_far_out, far_attn_out = after((grads[0], sum_far_out, far_attn_out))
    sum_far_out = swap_seq(sum_far_out, half)
    far_attn_out = swap_seq(far_attn_out, half)

    def back_of(group):
        out, lse = heads[group]
        return attend_back(queries, keys, values, grads[group], out, lse, cosine, sine, group)

    packed = [back_of(0)]
    packed[0], sum_far_out, far_attn_out = after((packed[0], sum_far_out, far_attn_out))
    output = (mixed + (sum_near_out + sum_far_out.astype(F32))).astype(BF16)
    grad_attn_out = (near_attn_out + far_attn_out.astype(F32)).astype(BF16)
    first_grads = jnp.concatenate(
        [dot_tn(x_all, packed[0]).astype(BF16), grad_attn_out], 1
    )
    sum_in = reduce_fsdp(grad_in)
    sum_mlp_out = reduce_fsdp(after((grad_mlp_out, grad_in))[0])
    for group in range(1, groups):
        grads[group], output, _, sum_in = after(
            (grads[group], output, first_grads, sum_in)
        )
        packed.append(back_of(group))
    reduced = [halve_fsdp(first_grads, 1, lambda got: after((got, packed[-1]))[0])]

    later_bits = [1 << at for at in range(1, fsdp_size.bit_length() - 1)]
    chains = [later_bits] + [[0, 1] + later_bits] * (groups - 1)
    far_grads = fold(token_grad(packed, qkv_weights, fsdp_size, half, positions, half))
    far_grads = far_grads.astype(BF16)
    reduced = reduced + [dot_tn(x_all, section).astype(BF16) for section in packed[1:]]
    cuts = [0, positions // 4, positions // 2, positions]
    near_grads, far_parts = None, None
    for stage in range(max(len(chain) for chain in chains)):
        if stage == 1:
            far_parts = [
                swap_seq(far_grads[start:end], half) for start, end in zip(cuts, cuts[1:])
            ]
            near_grads = token_grad(packed, qkv_weights, fsdp_size, half, positions, 0)
        if stage == 2:
            near_grads = fold(near_grads)
        reduced = [
            halve_fsdp(section, chain[stage])
            if stage < len(chain) and chain[stage]
            else section
            for section, chain in zip(reduced, chains)
        ]
        if stage == 0:
            reduced, far_grads, packed, sum_mlp_out = after(
                (reduced, far_grads, packed, sum_mlp_out)
            )
        if stage == 1:
            reduced, near_grads, far_parts[0] = after((reduced, near_grads, far_parts[0]))
        if stage == 2:
            reduced, near_grads, far_parts[1] = after((reduced, near_grads, far_parts[1]))
    if not isinstance(near_grads, jax.Array):
        near_grads = fold(near_grads)
    reduced = jnp.concatenate(reduced, 1)
    far_reduced = swap_seq(reduced, half)
    far_reduced, far_parts = after((far_reduced, far_parts))
    sum_mlp_out = after((sum_mlp_out, far_parts[0]))[0]
    normed_grad = jnp.concatenate(far_parts, 0).astype(F32) + near_grads
    d_input = (mixed_grad + norm_backward(normed_grad, xhat, inverse)).astype(BF16)

    in_pieces = by_member(gather_seq(sum_in))
    all_in = jnp.concatenate(
        [piece.reshape(shard, 2 * fsdp_size, unit_share) for piece in in_pieces], 2
    )
    all_in = all_in[:, :, :ff_shard].reshape(shard, -1).astype(F32)
    all_mlp_out = jnp.concatenate(by_member(gather_seq(sum_mlp_out)), 0)[:ff_shard].astype(F32)
    pieces = by_member(spread(reduced) + spread(far_reduced))
    section = 3 * lanes
    all_attn_out = jnp.concatenate(
        [piece[:, section : section + local_width] for piece in pieces], 1
    ).astype(F32)
    starts = [0] + [section * group + local_width for group in range(1, groups)]
    all_qkv = jnp.concatenate(
        [
            piece[:, start + part * lanes : start + (part + 1) * lanes]
            for part in range(3)
            for piece in pieces
            for start in starts
        ],
        1,
    ).astype(F32)
    grad_gain_attn = jnp.sum(all_qkv * w_qkv.astype(F32), 1)
    grad_gain_mlp = jnp.sum(all_in * w_in.astype(F32), 1)
    return (
        output.reshape(activations.shape),
        d_input.reshape(activations.shape),
        grad_gain_attn,
        grad_gain_mlp,
        all_qkv * own_gain_attn,
        all_attn_out,
        all_in * own_gain_mlp,
        all_mlp_out,
    )


def solution(mesh):
    in_specs = (
        P("fsdp", "seq", None),
        P("fsdp", "seq", None),
        P("fsdp"),
        P("fsdp", None),
        P("fsdp", None),
        P("fsdp"),
        P("fsdp", None),
        P("fsdp", None),
    )
    out_specs = (
        P("fsdp", "seq", None),
        P("fsdp", "seq", None),
        P("fsdp"),
        P("fsdp"),
        P("fsdp", None),
        P("fsdp", None),
        P("fsdp", None),
        P("fsdp", None),
    )
    body = functools.partial(local, mesh.shape["seq"], mesh.shape["fsdp"])
    return jax.shard_map(body, mesh=mesh, in_specs=in_specs, out_specs=out_specs, check_vma=False)
```
